32 devices in a mesh: stream: 8 (over z, x), cross: 4 (over y, core).
Axes of the slice: x: 2, y: 2, z: 4, core: 2. Of those that a mesh axis runs over, the one named last changes fastest.
Arguments:
- rhs: float32 [128, 320, 128], P(('stream', 'cross')), may hold values from -240 to 240
- damping: float32 [128, 320], P(('stream', 'cross')), may hold values from 3 to 6
- omega: float32 [1], replicated, may hold values from 1 to 3
- jac_diag: bfloat16 [128, 320, 320], P(('stream', 'cross')), may hold values from -0.15625 to 0.15625
- jac_face: bfloat16 [128, 320, 480], P(('stream', 'cross')), may hold values from -0.125 to 0.125
- face_list: int32 [128, 6], P(('stream', 'cross')), may hold values from 0 to 36, as said below
- stream_sends: int32 [32, 2, 4], P(('stream', 'cross')), may hold values from 0 to 19, as said below
- cross_sends: int32 [32, 2, 2], P(('stream', 'cross')), may hold values from 0 to 23, as said below
Outputs:
- solution: float32 [128, 320, 128], P(('stream', 'cross'))
- residual: float32 [128, 320, 128], P(('stream', 'cross'))
The draws below stay inside these ranges and needn't reach their ends.
Inputs may be any that keep to these rules, and one draw needn't show every extreme that they name: `face_list`: within each partition, each face of an element points to the opposite face of its neighbour: to a slot 6 e + f of an own element, to a received trace in the layout of the table, or to the zero last slot on radial boundaries. Every received slot is read by exactly one face. `stream_sends`: each row lists distinct own trace slots 6 e + f of streamwise faces, in the order in which the neighbour's table receives them. `cross_sends`: each row lists distinct own trace slots 6 e + f of azimuthal faces, in the order in which the neighbour's table receives them; the cross partitions close into a loop.
All inputs are finite; a program needn't handle non-finite values.
Results may differ from the reference program's by a relative error of at most 0.003.
The reference program's roundings to bfloat16 on the way count: a program that leaves them out, or rounds other values in their place, can miss the bound.
Values may be sent and summed in bfloat16 or wider, within the bound.
No kernel may reach another device: no remote copies, remote signals or barrier semaphores. Data moves between devices by JAX's collectives and lax.ppermute only.
A program may use at most 128 MiB of HBM per device.

```python
import math
import jax
import jax.numpy as jnp
import numpy as np
from jax import lax

NP = 4
NVAR = 5
COLS = 64
ES = 1
ER = 2
EA = 2
ITERS = 3
NU = 320
NT = 80
BLK = 128
E_DEV = 4
SS = 4
SC = 2
ELEMS = 128
N_STREAM = 8
N_CROSS = 4


def device_tables(order):
    cells = jnp.arange(E_DEV, dtype=jnp.int32)
    plane = ER * EA
    along = cells // plane
    radial = cells // EA % ER
    beside_all = cells % EA
    own = E_DEV * 6
    last_slot = own + 2 * SS + 2 * SC

    def slot(offset, face):
        return order[jnp.clip(cells + offset, 0, E_DEV - 1)] * 6 + face
    face_zero = jnp.where(along > 0, slot(-plane, 1), own + radial * EA + beside_all)
    face_one = jnp.where(along < ES - 1, slot(plane, 0), own + SS + radial * EA + beside_all)
    face_two = jnp.where(radial > 0, slot(-EA, 3), last_slot)
    face_three = jnp.where(radial < ER - 1, slot(EA, 2), last_slot)
    face_four = jnp.where(beside_all > 0, slot(-1, 5), own + 2 * SS + along * ER + radial)
    face_five = jnp.where(beside_all < EA - 1, slot(1, 4), own + 2 * SS + SC + along * ER + radial)
    geometric = jnp.stack([face_zero, face_one, face_two, face_three, face_four, face_five], axis=1)
    local = jnp.zeros((E_DEV, 6), jnp.int32).at[order].set(geometric.astype(jnp.int32))
    slab = jnp.arange(SS, dtype=jnp.int32)
    stream_rows = jnp.stack([order[(ES - 1) * plane + slab] * 6 + 1, order[slab] * 6], axis=0)
    ranks = jnp.arange(SC, dtype=jnp.int32)
    cross_rows = jnp.stack([order[ranks * EA + EA - 1] * 6 + 5, order[ranks * EA] * 6 + 4], axis=0)
    return (local, stream_rows.astype(jnp.int32), cross_rows.astype(jnp.int32))


def layout_tables(key):
    devices = N_STREAM * N_CROSS
    keys = jax.random.split(jax.random.fold_in(key, 23), devices)
    orders = jax.vmap(lambda item: jax.random.permutation(item, E_DEV).astype(jnp.int32))(keys)
    local, stream_rows, cross_rows = jax.vmap(device_tables)(orders)
    return (local.reshape(devices * E_DEV, 6), stream_rows, cross_rows)


def draw_face_list(key, part):
    return layout_tables(key)[0]


def draw_stream_sends(key, part):
    return layout_tables(key)[1]


def draw_cross_sends(key, part):
    return layout_tables(key)[2]


def draw_rhs(key, part):
    first, second, third = jax.random.split(jax.random.fold_in(key, 5), 3)
    element = jnp.arange(ELEMS)
    stream_index = element // E_DEV // N_CROSS
    ramp = 1.0 + 2.0 * stream_index.astype(jnp.float32) / max(N_STREAM - 1, 1)
    columns = jnp.exp(jax.random.uniform(second, (2 * COLS,), jnp.float32, 0.0, math.log(10.0)))
    rows = jnp.exp(jax.random.uniform(third, (ELEMS, NU), jnp.float32, 0.0, math.log(10.0)))
    base = jnp.clip(jax.random.normal(first, (ELEMS, NU, 2 * COLS), jnp.float32), -6.0, 6.0)
    return 0.1 * base * ramp[:, None, None] * rows[:, :, None] * columns[None, None, :]


def block_levels(rng, extent, pieces, low, top_value):
    def one(axis_at, blocks):
        steps = jax.random.uniform(jax.random.fold_in(jax.random.fold_in(rng, 6), axis_at), (blocks,), jnp.float32, low / len(pieces), top_value / len(pieces))
        return jnp.repeat(jnp.exp(steps), extent[axis_at] // blocks).reshape((-1,) + (1,) * (len(extent) - axis_at - 1))

    loudness = one(*pieces[0])
    for cut in pieces[1:]:
        loudness = loudness * one(*cut)
    return loudness


def noise(stream_key, shape, deviation, limit, cuts=(), held_as=jnp.bfloat16):
    drawn = jax.random.normal(stream_key, shape, jnp.float32) * deviation
    if len(cuts) > 0:
        drawn = block_levels(stream_key, shape, cuts, -0.22, 0.18) * drawn
    return jnp.clip(drawn, min=-limit, max=limit).astype(held_as)


def setup_inputs(seed: int = 0) -> dict:
    seeds = jax.random.split(jax.random.key(seed), 9)
    return {
        "rhs": draw_rhs(jax.random.fold_in(seeds[8], 71), 0),
        "damping": jnp.clip(jnp.exp(math.log(6.0) - 0.6931472 * jax.random.uniform(seeds[1], (ELEMS, NU), jnp.float32) ** block_levels(seeds[1], (ELEMS, NU), ((0, 32),), -0.2, 0.2)), 3.0, 6.0),
        "omega": jnp.clip(jax.random.uniform(seeds[2], (1,), jnp.float32, 1.0, 3.0), 1.0, 3.0),
        "jac_diag": noise(seeds[3], (ELEMS, NU, NU), (4 * NU) ** -0.5, 0.15625, ((0, 32),)),
        "jac_face": noise(seeds[4], (ELEMS, NU, 6 * NT), (24 * NT) ** -0.5, 0.125, ((0, 32),)),
        "face_list": draw_face_list(jax.random.fold_in(seeds[8], 71), 0),
        "stream_sends": draw_stream_sends(jax.random.fold_in(seeds[8], 71), 0),
        "cross_sends": draw_cross_sends(jax.random.fold_in(seeds[8], 71), 0),
    }


def inner(left, right):
    width = left.shape[-1] // 2
    return lax.dot_general(left.reshape(-1, width).astype(jnp.float32), right.reshape(-1, width).astype(jnp.float32), (((0,), (0,)), ((), ())), precision=lax.Precision.HIGHEST, preferred_element_type=jnp.float32)

def combine(field, matrix):
    width = matrix.shape[0]
    flat = field.reshape(-1, width)
    return jnp.dot(flat.astype(jnp.float32), matrix.astype(jnp.float32), precision=lax.Precision.HIGHEST, preferred_element_type=jnp.float32).reshape(field.shape)

def orthonormal(field, gram):
    lower = jnp.linalg.cholesky(gram)
    inverse = lax.linalg.triangular_solve(lower, jnp.eye(gram.shape[0], dtype=gram.dtype), left_side=True, lower=True)
    return (combine(field, inverse.T), lower.T)

def face_rows():
    grid = np.arange(NVAR * NP * NP * NP).reshape(NVAR, NP, NP, NP)
    faces = [grid[:, 0], grid[:, NP - 1], grid[:, :, 0], grid[:, :, NP - 1], grid[:, :, :, 0], grid[:, :, :, NP - 1]]
    return np.concatenate([item.reshape(-1) for item in faces]).astype(np.int32)

def face_traces(rounded):
    count = rounded.shape[0]
    columns = rounded.shape[-1]
    picked = jnp.take(rounded, jnp.asarray(face_rows()), axis=1)
    return picked.reshape(count * 6, NVAR * NP * NP, columns)

def rotate(field):
    half = field.shape[-1] // 2
    return jnp.concatenate([-field[..., half:], field[..., :half]], axis=-1)

def start_block(rhs):
    width = rhs.shape[-1] // 2
    real_part = rhs[..., :width]
    imag_part = rhs[..., width:]
    return jnp.concatenate([real_part, -imag_part, imag_part, real_part], axis=-1)

def least_squares(hessenberg, first_upper):
    height = hessenberg.shape[0]
    width = first_upper.shape[0]
    target = jnp.zeros((height, width), first_upper.dtype).at[:width].set(first_upper)
    normal = jnp.dot(hessenberg.T.astype(jnp.float32), hessenberg.astype(jnp.float32), precision=lax.Precision.HIGHEST, preferred_element_type=jnp.float32)
    right = jnp.dot(hessenberg.T.astype(jnp.float32), target.astype(jnp.float32), precision=lax.Precision.HIGHEST, preferred_element_type=jnp.float32)
    lower = jnp.linalg.cholesky(normal)
    middle = lax.linalg.triangular_solve(lower, right, left_side=True, lower=True)
    coeffs = lax.linalg.triangular_solve(lower, middle, left_side=True, lower=True, transpose_a=True)
    leftover = target - jnp.dot(hessenberg.astype(jnp.float32), coeffs.astype(jnp.float32), precision=lax.Precision.HIGHEST, preferred_element_type=jnp.float32)
    return (coeffs, leftover)

def reference(rhs, damping, omega, jac_diag, jac_face, face_list, stream_sends, cross_sends):
    devices = N_STREAM * N_CROSS
    columns = rhs.shape[-1] * 2
    diag_dev = jac_diag.reshape(devices, E_DEV, NU, NU)
    face_dev = jac_face.reshape(devices, E_DEV, NU, 6 * NT)
    list_dev = face_list.reshape(devices, E_DEV * 6)

    def apply_operator(field):
        rounded = field.astype(jnp.bfloat16)
        rounded_dev = rounded.reshape(devices, E_DEV, NU, columns)

        def packets(items):
            block, stream_rows, cross_rows = items
            traces = face_traces(block)
            return (traces[stream_rows], traces[cross_rows])
        stream_packs, cross_packs = lax.map(packets, (rounded_dev, stream_sends, cross_sends))
        grid = stream_packs.reshape(N_STREAM, N_CROSS, 2, SS, NT, columns)
        empty = jnp.zeros_like(grid[:1, :, 0])
        from_prev = jnp.concatenate([empty, grid[:-1, :, 0]], axis=0).reshape(devices, SS, NT, columns)
        from_next = jnp.concatenate([grid[1:, :, 1], empty], axis=0).reshape(devices, SS, NT, columns)
        cgrid = cross_packs.reshape(N_STREAM, N_CROSS, 2, SC, NT, columns)
        cross_prev = jnp.roll(cgrid[:, :, 0], 1, axis=1).reshape(devices, SC, NT, columns)
        cross_next = jnp.roll(cgrid[:, :, 1], -1, axis=1).reshape(devices, SC, NT, columns)

        def couple(items):
            block, diag_blocks, face_blocks, listing, first, second, third, fourth = items
            traces = face_traces(block)
            zero_slot = jnp.zeros((1, NT, columns), traces.dtype)
            table = jnp.concatenate([traces, first, second, third, fourth, zero_slot], axis=0)
            gathered = table[listing].reshape(E_DEV, 6 * NT, columns)
            interior = jnp.einsum('eij,ejc->eic', diag_blocks.astype(jnp.float32), block.astype(jnp.float32))
            coupled = jnp.einsum('eik,ekc->eic', face_blocks.astype(jnp.float32), gathered.astype(jnp.float32))
            return interior + coupled
        jacobian = lax.map(couple, (rounded_dev, diag_dev, face_dev, list_dev, from_prev, from_next, cross_prev, cross_next))
        jacobian = jacobian.reshape(field.shape)
        return jacobian + damping[:, :, None] * field + omega[0] * rotate(field)
    block = start_block(rhs)
    first, first_upper = orthonormal(block, inner(block, block))
    basis = [first]
    hessenberg = jnp.zeros(((ITERS + 1) * BLK, ITERS * BLK), jnp.float32)
    for step in range(ITERS):
        image = apply_operator(basis[step])
        coeffs = [inner(vector, image) for vector in basis]
        for number, vector in enumerate(basis):
            image = image - combine(vector, coeffs[number])
        fresh, upper = orthonormal(image, inner(image, image))
        for number in range(step + 1):
            hessenberg = hessenberg.at[number * BLK:(number + 1) * BLK, step * BLK:(step + 1) * BLK].set(coeffs[number])
        hessenberg = hessenberg.at[(step + 1) * BLK:(step + 2) * BLK, step * BLK:(step + 1) * BLK].set(upper)
        basis.append(fresh)
    weights, leftover = least_squares(hessenberg, first_upper)
    result = combine(basis[0], weights[:BLK])
    for step in range(1, ITERS):
        result = result + combine(basis[step], weights[step * BLK:(step + 1) * BLK])
    remain = combine(basis[0], leftover[:BLK])
    for step in range(1, ITERS + 1):
        remain = remain + combine(basis[step], leftover[step * BLK:(step + 1) * BLK])
    width = rhs.shape[-1] // 2
    solution = jnp.concatenate([result[..., :width], result[..., BLK:BLK + width]], axis=-1)
    residual = jnp.concatenate([remain[..., :width], remain[..., BLK:BLK + width]], axis=-1)
    return (solution, residual)
```

```python
import functools
import jax
import jax.numpy as jnp
import numpy as np
from jax import lax
from jax.experimental import pallas as pl
from jax.experimental.pallas import tpu as pltpu
from jax.sharding import PartitionSpec as P

NP = 4
NVAR = 5
ITERS = 3
FACES = 6
AXES = ("stream", "cross")
HIGH = lax.Precision.HIGHEST
F32 = jnp.float32
BF16 = jnp.bfloat16


def passed_along(value, axis, steps):
    count = lax.axis_size(axis)
    first, last = (max(0, -steps), min(count, count - steps))
    return lax.ppermute(value, axis, [(source, source + steps) for source in range(first, last)])


def shifted(block, axis, distance):
    devices = range(lax.axis_size(axis))
    route = [((i - distance) % len(devices), i) for i in devices]
    return lax.ppermute(block, axis, route)


def total(block):
    count = lax.axis_size(AXES[0]) * lax.axis_size(AXES[1])
    rows, width = block.shape
    share = -(-rows // count)
    if share * count != rows:
        block = jnp.pad(block, ((0, share * count - rows), (0, 0)))
    parts = lax.all_to_all(block.reshape(count, share, width), AXES, 0, 0)
    mine = jnp.broadcast_to(parts.sum(0)[None], parts.shape)
    return lax.all_to_all(mine, AXES, 0, 0).reshape(count * share, width)[:rows]


def mm(left, right):
    return jnp.dot(left, right, precision=HIGH, preferred_element_type=F32)


def mm_tn(left, right):
    return lax.dot_general(
        left, right, (((0,), (0,)), ((), ())), precision=HIGH, preferred_element_type=F32
    )


def mm_nt(left, right):
    return lax.dot_general(
        left, right, (((1,), (1,)), ((), ())), precision=HIGH, preferred_element_type=F32
    )


def grid_of(shape, axis):
    return lax.broadcasted_iota(jnp.int32, shape, axis)


def identity(size):
    return jnp.where(grid_of((size, size), 0) == grid_of((size, size), 1), 1.0, 0.0).astype(F32)


def factor(gram, work):
    size = gram.shape[0]
    step = 8
    work[:, :size] = gram
    work[:, size:] = identity(size)
    row = grid_of((step, 2 * size), 0)
    for base in range(0, size, step):
        panel = work[base : base + step, :]
        for t in range(step):
            column = panel[:, base + t : base + t + 1]
            pivot = column[t : t + 1, :]
            scale = lax.rsqrt(pivot)
            scale = scale * (1.5 - 0.5 * pivot * scale * scale)
            lead = panel[t : t + 1, :] * scale
            below = panel - (column * scale) * lead
            panel = jnp.where(row == t, lead, jnp.where(row > t, below, panel))
        work[base : base + step, :] = panel
        rest = base + step
        if rest < size:
            work[rest:, :] = work[rest:, :] - mm_tn(panel[:, rest:size], panel)
    upper = work[:, :size]
    upper = jnp.where(grid_of((size, size), 1) >= grid_of((size, size), 0), upper, 0.0)
    return upper, work[:, size:]


def halves(ref, element):
    width = ref.shape[-1] // 2
    return ref[element, :, :width], ref[element, :, width:]


def send_traces(rounded, element, picks_ref, traces_ref):
    size = traces_ref.shape[1]
    picked = jnp.dot(picks_ref[...], rounded, preferred_element_type=F32).astype(BF16)
    for face in range(FACES):
        traces_ref[element * FACES + face] = picked[face * size : (face + 1) * size, :]


def pack(sends_ref, traces_ref, out_ref):
    for row in range(out_ref.shape[0]):
        for item in range(out_ref.shape[1]):
            out_ref[row, item] = traces_ref[sends_ref[0, row, item]]


def start_gram_kernel(rhs_ref, damping_ref, out_ref):
    count, rows, width = rhs_ref.shape
    field = rhs_ref[...].reshape(count * rows, width)
    gram = mm_tn(field, field)
    mass = jnp.sum(jnp.sum(damping_ref[...], axis=1, keepdims=True), axis=0, keepdims=True)
    corner = (grid_of(gram.shape, 0) == width - 1) & (grid_of(gram.shape, 1) == 0)
    out_ref[...] = jnp.where(corner, mass, gram)


def start_kernel(
    cells, gram_ref, rhs_ref, picks_ref, ssend_ref, csend_ref,
    field_ref, traces_ref, sout_ref, cout_ref, upper_ref, inverse_ref, center_ref, work,
):
    count, rows, width = rhs_ref.shape
    half = width // 2
    raw = gram_ref[...]
    r, c = grid_of(raw.shape, 0), grid_of(raw.shape, 1)
    corner = (r == width - 1) & (c == 0)
    mass = raw[width - 1 : width, 0:1]
    raw = jnp.where(corner, raw[0:1, width - 1 : width], raw)
    center_ref[...] = jnp.broadcast_to(mass * (1.0 / cells), center_ref.shape)
    rr, ri = raw[:half, :half], raw[:half, half:]
    ir, ii = raw[half:, :half], raw[half:, half:]
    same, other = rr + ii, ir - ri
    gram = jnp.concatenate(
        [jnp.concatenate([same, other], 1), jnp.concatenate([-other, same], 1)], 0
    )
    upper, inverse = factor(gram, work)
    upper_ref[...] = upper
    inverse_ref[...] = inverse
    turn = inverse.T
    first = jnp.concatenate([turn[:half], -turn[half:]], 0)
    second = jnp.concatenate([turn[half:], turn[:half]], 0)
    wide = jnp.concatenate([first, second], 1)
    for e in range(count):
        field = mm(rhs_ref[e], wide)
        field_ref[e] = field
        send_traces(field.astype(BF16), e, picks_ref, traces_ref)
    pack(ssend_ref, traces_ref, sout_ref)
    pack(csend_ref, traces_ref, cout_ref)


def next_kernel(
    level, red_ref, image_ref, *refs,
):
    basis = refs[: level + 1]
    picks_ref, ssend_ref, csend_ref = refs[level + 1 : level + 4]
    field_ref, traces_ref, sout_ref, cout_ref, upper_ref, inverse_ref, work = refs[level + 4 :]
    width = red_ref.shape[-1]
    coeffs = [red_ref[j * width : (j + 1) * width, :] for j in range(level + 1)]
    gram = red_ref[(level + 1) * width : (level + 2) * width, :]
    for h in coeffs:
        gram = gram - mm_tn(h, h)
    upper, inverse = factor(gram, work)
    upper_ref[...] = upper
    inverse_ref[...] = inverse
    turn = inverse.T
    matrix = jnp.concatenate([turn] + [-mm(h, turn) for h in coeffs], 0)
    for e in range(image_ref.shape[0]):
        parts = [halves(ref, e) for ref in (image_ref,) + basis]
        field = jnp.concatenate(
            [mm(jnp.concatenate([p[h] for p in parts], 1), matrix) for h in range(2)], 1
        )
        field_ref[e] = field
        send_traces(field.astype(BF16), e, picks_ref, traces_ref)
    pack(ssend_ref, traces_ref, sout_ref)
    pack(csend_ref, traces_ref, cout_ref)


def turned(matrix):
    half = matrix.shape[0] // 2
    return jnp.concatenate([-matrix[half:], matrix[:half]], 0)


def inner_part(omega_ref, center_ref, damping_ref, diag_ref, field_ref, part_ref, twist):
    width = twist.shape[0]
    omega = omega_ref[0]
    center = center_ref[0:1, 0:1]
    offset = damping_ref[...] - center
    count = field_ref.shape[0]
    for e in range(count):
        re, im = halves(field_ref, e)
        rounded = field_ref[e].astype(BF16)
        local = jnp.dot(diag_ref[e], rounded, preferred_element_type=F32)
        scale = jnp.swapaxes(offset[e : e + 1, :], 0, 1)
        part_ref[e, :, :width] = local[:, :width] + scale * re - omega * im - mm(re, twist)
        part_ref[e, :, width:] = local[:, width:] + scale * im + omega * re - mm(im, twist)


def first_inner_kernel(
    omega_ref, center_ref, damping_ref, diag_ref, field_ref, upper_ref, inverse_ref,
    part_ref, shift_ref,
):
    twist = omega_ref[0] * mm(upper_ref[...], turned(inverse_ref[...].T))
    shift_ref[...] = twist + center_ref[0:1, 0:1] * identity(twist.shape[0])
    inner_part(omega_ref, center_ref, damping_ref, diag_ref, field_ref, part_ref, twist)


def inner_kernel(
    omega_ref, center_ref, damping_ref, diag_ref, field_ref, upper_ref, inverse_ref,
    chain_ref, unchain_ref,
    part_ref, shift_ref, chain_out, unchain_out,
):
    chain = mm(upper_ref[...], chain_ref[...])
    unchain = mm_nt(unchain_ref[...], inverse_ref[...])
    chain_out[...] = chain
    unchain_out[...] = unchain
    twist = omega_ref[0] * mm(chain, turned(unchain))
    shift_ref[...] = twist + center_ref[0:1, 0:1] * identity(twist.shape[0])
    inner_part(omega_ref, center_ref, damping_ref, diag_ref, field_ref, part_ref, twist)


def square_kernel(
    h00_ref, h01_ref, h11_ref, s0_ref, i1_ref, i2_ref,
    n1_ref, n2_ref, ip_ref, rhs_ref, work,
):
    n1 = -mm_nt(i1_ref[...], h00_ref[...])
    n2 = -mm(i2_ref[...], h01_ref[...].T + mm_tn(h11_ref[...], n1))
    gram = identity(n1.shape[0]) + mm_tn(n1, n1) + mm_tn(n2, n2)
    _, inverse = factor(gram, work)
    n1_ref[...] = n1
    n2_ref[...] = n2
    ip_ref[...] = inverse
    rhs_ref[...] = mm(inverse, s0_ref[...])


def outer_kernel(level, list_ref, traces_ref, prev_ref, next_ref, cprev_ref, cnext_ref,
                 face_ref, part_ref, *refs):
    basis = refs[: level + 1]
    image_ref, out_ref, table, nearby = refs[level + 1 :]
    own = traces_ref.shape[0]
    size = traces_ref.shape[1]
    at = 0
    for ref in (traces_ref, prev_ref, next_ref, cprev_ref, cnext_ref):
        table[at : at + ref.shape[0]] = ref[...]
        at += ref.shape[0]
    table[at] = jnp.zeros(table.shape[1:], table.dtype)
    count = face_ref.shape[0]
    width = part_ref.shape[-1] // 2
    for e in range(count):
        for f in range(FACES):
            nearby[f * size : (f + 1) * size, :] = table[list_ref[e, f]]
        coupled = jnp.dot(face_ref[e], nearby[...], preferred_element_type=F32)
        image_ref[e] = part_ref[e] + coupled
    sums = None
    rows = image_ref.shape[1]
    for h in range(2):
        cut = slice(h * width, (h + 1) * width)
        image = image_ref[:, :, cut].reshape(count * rows, width)
        stack = [ref[:, :, cut].reshape(count * rows, width) for ref in basis] + [image]
        term = mm_tn(jnp.concatenate(stack, 1), image)
        sums = term if sums is None else sums + term
    out_ref[...] = sums


def final_kernel(
    red_ref, image_ref, v0_ref, v1_ref, v2_ref, shift2_ref, h11_ref, h01_ref, h00_ref,
    i1_ref, i2_ref, n1_ref, n2_ref, ip_ref, rhs_ref, s0_ref,
    solution_ref, residual_ref, work,
):
    width = red_ref.shape[-1]
    half = width // 2
    g0, g1, g2, gram = [red_ref[j * width : (j + 1) * width, :] for j in range(4)]
    h02, h12, h22 = g0, g1, g2 + shift2_ref[...]
    for g in (g0, g1, g2):
        gram = gram - mm_tn(g, g)
    n1, n2, ip = n1_ref[...], n2_ref[...], ip_ref[...]
    reach = h02.T + mm_tn(h12, n1) + mm_tn(h22, n2)
    reach = mm_nt(reach, ip)
    _, iq = factor(gram + mm_nt(reach, reach), work)
    right = rhs_ref[...]
    y2 = mm_tn(iq, mm(iq, mm(reach, right)))
    z0 = mm_tn(ip, right - mm_tn(reach, y2))
    z1 = mm(n1, z0)
    z2 = mm(n2, z0)
    y1 = -mm_tn(i2_ref[...], z2 + mm(h22, y2))
    y0 = -mm_tn(i1_ref[...], z1 + mm(h11_ref[...], y1) + mm(h12, y2))
    left = grid_of((width, width), 1) < half
    rows = []
    for y, z in ((y0, z0 + mm(g0, y2)), (y1, z1 + mm(g1, y2)), (y2, z2 + mm(g2, y2)), (0.0 * y2, -y2)):
        rows.append(jnp.where(left, y, pltpu.roll(z, half, 1)))
    matrix = jnp.concatenate(rows, 0)
    lanes = grid_of((image_ref.shape[1], width), 1) < half
    for e in range(image_ref.shape[0]):
        parts = [halves(ref, e) for ref in (v0_ref, v1_ref, v2_ref, image_ref)]
        first, second = [mm(jnp.concatenate([p[h] for p in parts], 1), matrix) for h in range(2)]
        solution_ref[e] = jnp.where(lanes, first, pltpu.roll(second, half, 1))
        residual_ref[e] = jnp.where(lanes, pltpu.roll(first, half, 1), second)


def face_rows():
    grid = np.arange(NVAR * NP * NP * NP).reshape(NVAR, NP, NP, NP)
    faces = [
        grid[:, 0],
        grid[:, NP - 1],
        grid[:, :, 0],
        grid[:, :, NP - 1],
        grid[:, :, :, 0],
        grid[:, :, :, NP - 1],
    ]
    return np.concatenate([item.reshape(-1) for item in faces]).astype(np.int32)


VM = pl.BlockSpec(memory_space=pltpu.VMEM)
SM = pl.BlockSpec(memory_space=pltpu.SMEM)


def call(kernel, name, args, outs, scratch=(), scalars=(), flops=0):
    specs = [SM if i in scalars else VM for i in range(len(args))]
    bytes_moved = sum(a.size * a.dtype.itemsize for a in args)
    return pl.pallas_call(
        kernel,
        name=name,
        out_shape=[jax.ShapeDtypeStruct(shape, dtype) for shape, dtype in outs],
        in_specs=specs,
        out_specs=[VM] * len(outs),
        scratch_shapes=list(scratch),
        cost_estimate=pl.CostEstimate(flops=flops, bytes_accessed=bytes_moved, transcendentals=0),
    )(*args)


def body(rhs, damping, omega, jac_diag, jac_face, face_list, stream_sends, cross_sends):
    count, rows, blocksize = rhs.shape
    columns = 2 * blocksize
    size = NVAR * NP * NP
    slots = count * FACES
    ss, sc = stream_sends.shape[-1], cross_sends.shape[-1]
    devices = lax.axis_size("stream") * lax.axis_size("cross")
    picks = np.zeros((FACES * size, rows), np.float32)
    picks[np.arange(FACES * size), face_rows()] = 1.0
    picks = jnp.asarray(picks, BF16)
    square = ((blocksize, blocksize), F32)
    field_out = ((count, rows, columns), F32)
    work = pltpu.VMEM((blocksize, 2 * blocksize), F32)
    stage = [
        field_out,
        ((slots, size, columns), BF16),
        ((2, ss, size, columns), BF16),
        ((2, sc, size, columns), BF16),
        square,
        square,
    ]

    (gram,) = call(start_gram_kernel, "start_gram", [rhs, damping], [square])
    gram = total(gram)
    cells = float(devices * count * rows)
    field, traces, spack, cpack, upper, inverse, center = call(
        functools.partial(start_kernel, cells),
        "start",
        [gram, rhs, picks, stream_sends, cross_sends],
        stage + [((8, blocksize), F32)],
        [work],
        (3, 4),
    )
    basis = [field]
    uppers, inverses = [upper], [inverse]
    hess = {}
    chain, unchain = upper, None
    for step in range(ITERS):
        from_prev = passed_along(spack[0], "stream", 1)
        from_next = passed_along(spack[1], "stream", -1)
        cross_prev = shifted(cpack[0], "cross", 1)
        cross_next = shifted(cpack[1], "cross", -1)
        common = [omega, center, damping, jac_diag, field, upper, inverse]
        if step == 0:
            part, shift = call(
                first_inner_kernel, "inner", common, [field_out, square], (), (0,), 10**9
            )
            unchain = inverse.T
        else:
            part, shift, chain, unchain = call(
                inner_kernel,
                "inner",
                common + [chain, unchain],
                [field_out, square, square, square],
                (),
                (0,),
                10**9,
            )
        if step == ITERS - 1:
            n1, n2, ip, right = call(
                square_kernel,
                "square",
                [hess[0, 0], hess[0, 1], hess[1, 1], uppers[0], inverses[1], inverses[2]],
                [square] * 4,
                [work],
                (),
                10**9,
            )
        image, sums = call(
            functools.partial(outer_kernel, step),
            "outer",
            [face_list, traces, from_prev, from_next, cross_prev, cross_next, jac_face, part]
            + basis,
            [field_out, (((step + 2) * blocksize, blocksize), F32)],
            [
                pltpu.VMEM((slots + 2 * ss + 2 * sc + 1, size, columns), BF16),
                pltpu.VMEM((FACES * size, columns), BF16),
            ],
            (0,),
        )
        sums = total(sums)
        if step < ITERS - 1:
            for j in range(step + 1):
                hess[j, step] = sums[j * blocksize : (j + 1) * blocksize]
            hess[step, step] = hess[step, step] + shift
            field, traces, spack, cpack, upper, inverse = call(
                functools.partial(next_kernel, step),
                "next",
                [sums, image] + basis + [picks, stream_sends, cross_sends],
                stage,
                [work],
                (step + 4, step + 5),
            )
            basis.append(field)
            uppers.append(upper)
            inverses.append(inverse)
    out = ((count, rows, blocksize), F32)
    return tuple(
        call(
            final_kernel,
            "final",
            [sums, image] + basis
            + [shift, hess[1, 1], hess[0, 1], hess[0, 0], inverses[1], inverses[2]]
            + [n1, n2, ip, right, uppers[0]],
            [out, out],
            [work],
        )
    )


def solution(mesh):
    in_specs = (
        P(("stream", "cross"), None, None),
        P(("stream", "cross"), None),
        P(),
        P(("stream", "cross"), None, None),
        P(("stream", "cross"), None, None),
        P(("stream", "cross"), None),
        P(("stream", "cross"), None, None),
        P(("stream", "cross"), None, None),
    )
    out_specs = (P(("stream", "cross"), None, None), P(("stream", "cross"), None, None))
    return jax.shard_map(body, mesh=mesh, in_specs=in_specs, out_specs=out_specs, check_vma=False)
```

```python
import functools
import jax
import jax.numpy as jnp
import numpy as np
from jax import lax
from jax.experimental import pallas as pl
from jax.experimental.pallas import tpu as pltpu
from jax.sharding import PartitionSpec as P

NP = 4
NVAR = 5
ITERS = 3
FACES = 6
AXES = ("stream", "cross")
HIGH = lax.Precision.HIGHEST
F32 = jnp.float32
BF16 = jnp.bfloat16
LANES = 128
VMEM_LIMIT = 20 * 2**20


def passed_along(value, axis, steps):
    count = lax.axis_size(axis)
    first, last = (max(0, -steps), min(count, count - steps))
    return lax.ppermute(value, axis, [(source, source + steps) for source in range(first, last)])


def shifted(block, axis, distance):
    devices = range(lax.axis_size(axis))
    route = [((i - distance) % len(devices), i) for i in devices]
    return lax.ppermute(block, axis, route)


def total(block):
    count = lax.axis_size(AXES[0]) * lax.axis_size(AXES[1])
    rows, width = block.shape
    share = -(-rows // count)
    if share * count != rows:
        block = jnp.pad(block, ((0, share * count - rows), (0, 0)))
    parts = lax.all_to_all(block.reshape(count, share, width), AXES, 0, 0)
    (mine,) = call(add_up_kernel, "add_up", [parts], [(parts.shape, F32)], limit=4 * 2**20)
    return lax.all_to_all(mine, AXES, 0, 0).reshape(count * share, width)[:rows]


def mm(left, right):
    return jnp.dot(left, right, precision=HIGH, preferred_element_type=F32)


def mm_tn(left, right):
    return lax.dot_general(
        left, right, (((0,), (0,)), ((), ())), precision=HIGH, preferred_element_type=F32
    )


def mm_nt(left, right):
    return lax.dot_general(
        left, right, (((1,), (1,)), ((), ())), precision=HIGH, preferred_element_type=F32
    )


def grid_of(shape, axis):
    return lax.broadcasted_iota(jnp.int32, shape, axis)


def identity(size):
    return jnp.where(grid_of((size, size), 0) == grid_of((size, size), 1), 1.0, 0.0).astype(F32)


def pivot_block(corner):
    size = corner.shape[0]
    columns = [jnp.broadcast_to(corner[:, t : t + 1], (size, LANES)) for t in range(size)]
    left = [[jnp.broadcast_to(columns[j][i : i + 1], (size, LANES)) for j in range(i + 1)] for i in range(size)]
    lower = [[None] * size for _ in range(size)]
    scales = []
    for j in range(size):
        scales.append(lax.rsqrt(left[j][j]))
        for i in range(j + 1, size):
            lower[i][j] = left[i][j] * scales[j]
        for i in range(j + 1, size):
            for k in range(j + 1, i + 1):
                left[i][k] = left[i][k] - lower[i][j] * lower[k][j]
    return lower, scales


def factor(gram):
    size = gram.shape[0]
    step = 8
    unit = identity(size)
    sides = [[m[r : r + step] for r in range(0, size, step)] for m in (gram, unit)]
    row = grid_of((step, size), 0)
    for p in range(size // step):
        base = p * step
        lower, scales = pivot_block(sides[0][p][:, base : base + step])
        leads = []
        for side in sides:
            rows = [jnp.broadcast_to(side[p][t : t + 1], (step, size)) for t in range(step)]
            for t in range(step):
                rows[t] = rows[t] * scales[t]
                for u in range(t + 1, step):
                    rows[u] = rows[u] - lower[u][t] * rows[t]
            strip = rows[0]
            for t in range(1, step):
                strip = jnp.where(row == t, rows[t], strip)
            side[p] = strip
            leads.append(rows)
        for q in range(p + 1, size // step):
            strip = sides[0][q]
            columns = [jnp.broadcast_to(strip[:, base + t : base + t + 1], (step, size)) for t in range(step)]
            for t in range(step):
                share = columns[t] * scales[t]
                for u in range(t + 1, step):
                    columns[u] = columns[u] - share * lower[u][t]
                for side, lead in zip(sides, leads):
                    side[q] = side[q] - share * lead[t]
    upper = jnp.concatenate(sides[0], 0)
    upper = jnp.where(grid_of((size, size), 1) >= grid_of((size, size), 0), upper, 0.0)
    return upper, jnp.concatenate(sides[1], 0)


def halves(ref, element):
    width = ref.shape[-1] // 2
    return ref[element, :, :width], ref[element, :, width:]


def send_traces(rounded, element, picks_ref, traces_ref):
    size = traces_ref.shape[1]
    picked = jnp.dot(picks_ref[...], rounded, preferred_element_type=F32).astype(BF16)
    for face in range(FACES):
        traces_ref[element * FACES + face] = picked[face * size : (face + 1) * size, :]


def pack(sends_ref, traces_ref, out_refs):
    for row, out_ref in enumerate(out_refs):
        for item in range(out_ref.shape[0]):
            out_ref[item] = traces_ref[sends_ref[0, row, item]]


def add_up_kernel(parts_ref, out_ref):
    out_ref[...] = jnp.broadcast_to(jnp.sum(parts_ref[...], axis=0, keepdims=True), out_ref.shape)


def start_gram_kernel(rhs_ref, damping_ref, out_ref):
    count, rows, width = rhs_ref.shape
    field = rhs_ref[...].reshape(count * rows, width)
    gram = mm_tn(field, field)
    mass = jnp.sum(jnp.sum(damping_ref[...], axis=1, keepdims=True), axis=0, keepdims=True)
    corner = (grid_of(gram.shape, 0) == width - 1) & (grid_of(gram.shape, 1) == 0)
    out_ref[...] = jnp.where(corner, mass, gram)


def start_kernel(
    cells, gram_ref, rhs_ref, picks_ref, ssend_ref, csend_ref,
    field_ref, traces_ref, s0_ref, s1_ref, c0_ref, c1_ref, upper_ref, inverse_ref, center_ref,
):
    count, rows, width = rhs_ref.shape
    half = width // 2
    raw = gram_ref[...]
    r, c = grid_of(raw.shape, 0), grid_of(raw.shape, 1)
    corner = (r == width - 1) & (c == 0)
    mass = raw[width - 1 : width, 0:1]
    raw = jnp.where(corner, raw[0:1, width - 1 : width], raw)
    center_ref[...] = jnp.broadcast_to(mass * (1.0 / cells), center_ref.shape)
    rr, ri = raw[:half, :half], raw[:half, half:]
    ir, ii = raw[half:, :half], raw[half:, half:]
    same, other = rr + ii, ir - ri
    gram = jnp.concatenate(
        [jnp.concatenate([same, other], 1), jnp.concatenate([-other, same], 1)], 0
    )
    upper, inverse = factor(gram)
    upper_ref[...] = upper
    inverse_ref[...] = inverse
    turn = inverse.T
    first = jnp.concatenate([turn[:half], -turn[half:]], 0)
    second = jnp.concatenate([turn[half:], turn[:half]], 0)
    wide = jnp.concatenate([first, second], 1)

    @pl.loop(0, count)
    def _(e):
        field = mm(rhs_ref[e], wide)
        field_ref[e] = field
        send_traces(field.astype(BF16), e, picks_ref, traces_ref)

    pack(ssend_ref, traces_ref, (s0_ref, s1_ref))
    pack(csend_ref, traces_ref, (c0_ref, c1_ref))


def next_kernel(
    level, red_ref, image_ref, *refs,
):
    basis = refs[: level + 1]
    picks_ref, ssend_ref, csend_ref = refs[level + 1 : level + 4]
    field_ref, traces_ref, s0_ref, s1_ref, c0_ref, c1_ref, upper_ref, inverse_ref = refs[level + 4 :]
    width = red_ref.shape[-1]
    coeffs = [red_ref[j * width : (j + 1) * width, :] for j in range(level + 1)]
    gram = red_ref[(level + 1) * width : (level + 2) * width, :]
    for h in coeffs:
        gram = gram - mm_tn(h, h)
    upper, inverse = factor(gram)
    upper_ref[...] = upper
    inverse_ref[...] = inverse
    turn = inverse.T
    matrix = jnp.concatenate([turn] + [-mm(h, turn) for h in coeffs], 0)

    @pl.loop(0, image_ref.shape[0])
    def _(e):
        parts = [halves(ref, e) for ref in (image_ref,) + basis]
        field = jnp.concatenate(
            [mm(jnp.concatenate([p[h] for p in parts], 1), matrix) for h in range(2)], 1
        )
        field_ref[e] = field
        send_traces(field.astype(BF16), e, picks_ref, traces_ref)

    pack(ssend_ref, traces_ref, (s0_ref, s1_ref))
    pack(csend_ref, traces_ref, (c0_ref, c1_ref))


def turned(matrix):
    half = matrix.shape[0] // 2
    return jnp.concatenate([-matrix[half:], matrix[:half]], 0)


def inner_kernel(
    omega_ref, center_ref, damping_ref, diag_ref, field_ref, upper_ref, inverse_ref, *refs,
):
    part_ref, shift_ref, chain_out, unchain_out = refs[-4:]
    chain_refs = refs[:-4]
    chain, unchain = upper_ref[...], inverse_ref[...].T
    if chain_refs:
        chain = mm(chain, chain_refs[0][...])
        unchain = mm(chain_refs[1][...], unchain)
    chain_out[...] = chain
    unchain_out[...] = unchain
    omega = omega_ref[0]
    center = center_ref[0:1, 0:1]
    twist = omega * mm(chain, turned(unchain))
    shift_ref[...] = twist + center * identity(twist.shape[0])
    width = twist.shape[0]

    @pl.loop(0, field_ref.shape[0])
    def _(e):
        re, im = halves(field_ref, e)
        rounded = field_ref[e].astype(BF16)
        local = jnp.dot(diag_ref[e], rounded, preferred_element_type=F32)
        scale = jnp.swapaxes(damping_ref[pl.ds(e, 1), :] - center, 0, 1)
        part_ref[e, :, :width] = local[:, :width] + scale * re - omega * im - mm(re, twist)
        part_ref[e, :, width:] = local[:, width:] + scale * im + omega * re - mm(im, twist)


def square_kernel(
    sums0_ref, sums1_ref, shift0_ref, shift1_ref, shift2_ref, s0_ref, i1_ref, i2_ref, pack_ref,
):
    width = s0_ref.shape[0]
    h00 = sums0_ref[:width, :] + shift0_ref[...]
    h01 = sums1_ref[:width, :]
    h11 = sums1_ref[width : 2 * width, :] + shift1_ref[...]
    n1 = -mm_nt(i1_ref[...], h00)
    n2 = -mm(i2_ref[...], h01.T + mm_tn(h11, n1))
    gram = identity(width) + mm_tn(n1, n1) + mm_tn(n2, n2)
    _, inverse = factor(gram)
    right = mm(inverse, s0_ref[...])
    for at, item in enumerate(
        (shift2_ref[...], h11, i1_ref[...], i2_ref[...], n1, n2, inverse, right)
    ):
        pack_ref[at] = item


def outer_kernel(level, list_ref, traces_ref, prev_ref, next_ref, cprev_ref, cnext_ref,
                 face_ref, part_ref, *refs):
    basis = refs[: level + 1]
    image_ref, out_ref, table, nearby = refs[level + 1 :]
    own = traces_ref.shape[0]
    size = traces_ref.shape[1]
    at = 0
    for ref in (traces_ref, prev_ref, next_ref, cprev_ref, cnext_ref):
        table[at : at + ref.shape[0]] = ref[...]
        at += ref.shape[0]
    table[at] = jnp.zeros(table.shape[1:], table.dtype)
    count, rows = face_ref.shape[:2]
    width = part_ref.shape[-1] // 2

    @pl.loop(0, count)
    def _(e):
        for f in range(FACES):
            nearby[f * size : (f + 1) * size, :] = table[list_ref[e, f]]
        coupled = jnp.dot(face_ref[e], nearby[...], preferred_element_type=F32)
        image_ref[e] = part_ref[e] + coupled

    used = (level + 2) * width
    out_ref[...] = jnp.zeros_like(out_ref)

    @pl.loop(0, 2)
    def _(h):
        cut = pl.ds(pl.multiple_of(h * width, width), width)
        image = image_ref[:, :, cut].reshape(count * rows, width)
        stack = [ref[:, :, cut].reshape(count * rows, width) for ref in basis] + [image]
        out_ref[:used, :] += mm_tn(jnp.concatenate(stack, 1), image)


def final_kernel(
    red_ref, image_ref, v0_ref, v1_ref, v2_ref, pack_ref, solution_ref, residual_ref,
    fields, small, solved, left_over, in_sems, out_sems,
):
    load = pltpu.make_async_copy(pack_ref, small, in_sems.at[4])
    load.start()
    loads = [
        pltpu.make_async_copy(ref, fields.at[j], in_sems.at[j])
        for j, ref in enumerate((v0_ref, v1_ref, v2_ref, image_ref))
    ]
    for copy in loads:
        copy.start()
    width = red_ref.shape[-1]
    half = width // 2
    g0, g1, g2, gram = [red_ref[j * width : (j + 1) * width, :] for j in range(4)]
    for g in (g0, g1, g2):
        gram = gram - mm_tn(g, g)
    load.wait()
    shift2, h11, i1, i2, n1, n2, ip, right = [small[k] for k in range(8)]
    h02, h12, h22 = g0, g1, g2 + shift2
    reach = h02.T + mm_tn(h12, n1) + mm_tn(h22, n2)
    reach = mm_nt(reach, ip)
    _, iq = factor(gram + mm_nt(reach, reach))
    y2 = mm_tn(iq, mm(iq, mm(reach, right)))
    z0 = mm_tn(ip, right - mm_tn(reach, y2))
    z1 = mm(n1, z0)
    z2 = mm(n2, z0)
    y1 = -mm_tn(i2, z2 + mm(h22, y2))
    y0 = -mm_tn(i1, z1 + mm(h11, y1) + mm(h12, y2))
    left = grid_of((width, width), 1) < half
    rows = []
    for y, z in ((y0, z0 + mm(g0, y2)), (y1, z1 + mm(g1, y2)), (y2, z2 + mm(g2, y2)), (0.0 * y2, -y2)):
        rows.append(jnp.where(left, y, pltpu.roll(z, half, 1)))
    matrix = jnp.concatenate(rows, 0)
    count, rows_here = solved.shape[:2]
    lanes = grid_of((rows_here, width), 1) < half
    for copy in loads:
        copy.wait()

    def copies(e):
        return [
            pltpu.make_async_copy(solved.at[e], solution_ref.at[e], out_sems.at[0, e]),
            pltpu.make_async_copy(left_over.at[e], residual_ref.at[e], out_sems.at[1, e]),
        ]

    @pl.loop(0, count)
    def _(e):
        parts = [halves(fields.at[j], e) for j in range(4)]
        first, second = [mm(jnp.concatenate([p[h] for p in parts], 1), matrix) for h in range(2)]
        solved[e] = jnp.where(lanes, first, pltpu.roll(second, half, 1))
        left_over[e] = jnp.where(lanes, pltpu.roll(first, half, 1), second)
        for copy in copies(e):
            copy.start()

    for e in range(count):
        for copy in copies(e):
            copy.wait()


def face_rows():
    grid = np.arange(NVAR * NP * NP * NP).reshape(NVAR, NP, NP, NP)
    faces = [
        grid[:, 0],
        grid[:, NP - 1],
        grid[:, :, 0],
        grid[:, :, NP - 1],
        grid[:, :, :, 0],
        grid[:, :, :, NP - 1],
    ]
    return np.concatenate([item.reshape(-1) for item in faces]).astype(np.int32)


VM = pl.BlockSpec(memory_space=pltpu.VMEM)
SM = pl.BlockSpec(memory_space=pltpu.SMEM)
AN = pl.BlockSpec(memory_space=pl.ANY)


def call(
    kernel, name, args, outs, scratch=(), scalars=(), flops=0, limit=VMEM_LIMIT, apart=(), out_apart=()
):
    moved = sum(a.size * a.dtype.itemsize for a in args)
    return pl.pallas_call(
        kernel,
        name=name,
        out_shape=[jax.ShapeDtypeStruct(shape, dtype) for shape, dtype in outs],
        in_specs=[SM if i in scalars else AN if i in apart else VM for i in range(len(args))],
        out_specs=[AN if i in out_apart else VM for i in range(len(outs))],
        scratch_shapes=list(scratch),
        compiler_params=pltpu.CompilerParams(vmem_limit_bytes=limit),
        cost_estimate=pl.CostEstimate(flops=flops, bytes_accessed=moved, transcendentals=0),
    )(*args)


def body(rhs, damping, omega, jac_diag, jac_face, face_list, stream_sends, cross_sends):
    count, rows, blocksize = rhs.shape
    columns = 2 * blocksize
    size = NVAR * NP * NP
    slots = count * FACES
    ss, sc = stream_sends.shape[-1], cross_sends.shape[-1]
    devices = lax.axis_size("stream") * lax.axis_size("cross")
    picks = np.zeros((FACES * size, rows), np.float32)
    picks[np.arange(FACES * size), face_rows()] = 1.0
    picks = jnp.asarray(picks, BF16)
    square = ((blocksize, blocksize), F32)
    field_out = ((count, rows, columns), F32)
    stage = [
        field_out,
        ((slots, size, columns), BF16),
        ((ss, size, columns), BF16),
        ((ss, size, columns), BF16),
        ((sc, size, columns), BF16),
        ((sc, size, columns), BF16),
        square,
        square,
    ]

    (gram,) = call(start_gram_kernel, "start_gram", [rhs, damping], [square])
    gram = total(gram)
    cells = float(devices * count * rows)
    field, traces, s0, s1, c0, c1, upper, inverse, center = call(
        functools.partial(start_kernel, cells),
        "start",
        [gram, rhs, picks, stream_sends, cross_sends],
        stage + [((8, blocksize), F32)],
        [],
        (3, 4),
    )
    basis, uppers, inverses, shifts, reduced = [field], [upper], [inverse], [], []
    chains = []
    for step in range(ITERS):
        from_prev = passed_along(s0, "stream", 1)
        from_next = passed_along(s1, "stream", -1)
        cross_prev = shifted(c0, "cross", 1)
        cross_next = shifted(c1, "cross", -1)
        part, shift, *chains = call(
            inner_kernel,
            "inner",
            [omega, center, damping, jac_diag, field, upper, inverse] + chains,
            [field_out, square, square, square],
            (),
            (0,),
            10**9,
        )
        shifts.append(shift)
        if step == ITERS - 1:
            (known,) = call(
                square_kernel,
                "square",
                reduced + shifts + [uppers[0], inverses[1], inverses[2]],
                [((8, blocksize, blocksize), F32)],
                (),
                (),
                10**9,
            )
        blocks = 2 if step == 0 else 4
        image, sums = call(
            functools.partial(outer_kernel, step),
            "outer",
            [face_list, traces, from_prev, from_next, cross_prev, cross_next, jac_face, part]
            + basis,
            [field_out, ((blocks * blocksize, blocksize), F32)],
            [
                pltpu.VMEM((slots + 2 * ss + 2 * sc + 1, size, columns), BF16),
                pltpu.VMEM((FACES * size, columns), BF16),
            ],
            (0,),
        )
        sums = total(sums)
        if step < ITERS - 1:
            reduced.append(sums)
            field, traces, s0, s1, c0, c1, upper, inverse = call(
                functools.partial(next_kernel, step),
                "next",
                [sums, image] + basis + [picks, stream_sends, cross_sends],
                stage,
                [],
                (step + 4, step + 5),
            )
            basis.append(field)
            uppers.append(upper)
            inverses.append(inverse)
    out = ((count, rows, blocksize), F32)
    return tuple(
        call(
            final_kernel,
            "final",
            [sums, image] + basis + [known],
            [out, out],
            [
                pltpu.VMEM((4,) + field_out[0], F32),
                pltpu.VMEM((8, blocksize, blocksize), F32),
                pltpu.VMEM(*out),
                pltpu.VMEM(*out),
                pltpu.SemaphoreType.DMA((5,)),
                pltpu.SemaphoreType.DMA((2, count)),
            ],
            (),
            0,
            None,
            range(1, 6),
            (0, 1),
        )
    )


def solution(mesh):
    in_specs = (
        P(("stream", "cross"), None, None),
        P(("stream", "cross"), None),
        P(),
        P(("stream", "cross"), None, None),
        P(("stream", "cross"), None, None),
        P(("stream", "cross"), None),
        P(("stream", "cross"), None, None),
        P(("stream", "cross"), None, None),
    )
    out_specs = (P(("stream", "cross"), None, None), P(("stream", "cross"), None, None))
    return jax.shard_map(body, mesh=mesh, in_specs=in_specs, out_specs=out_specs, check_vma=False)
```

```python
import functools
import jax
import jax.numpy as jnp
import numpy as np
from jax import lax
from jax.experimental import pallas as pl
from jax.experimental.pallas import tpu as pltpu
from jax.sharding import PartitionSpec as P

NP = 4
NVAR = 5
ITERS = 3
FACES = 6
AXES = ("stream", "cross")
HIGH = lax.Precision.HIGHEST
F32 = jnp.float32
BF16 = jnp.bfloat16
LANES = 128
NEAR = 4
VMEM_LIMIT = 20 * 2**20


def passed_along(value, axis, steps):
    count = lax.axis_size(axis)
    first, last = (max(0, -steps), min(count, count - steps))
    return lax.ppermute(value, axis, [(source, source + steps) for source in range(first, last)])


def shifted(block, axis, distance):
    devices = range(lax.axis_size(axis))
    route = [((i - distance) % len(devices), i) for i in devices]
    return lax.ppermute(block, axis, route)


def total(block):
    count = lax.axis_size(AXES[0]) * lax.axis_size(AXES[1])
    rows, width = block.shape
    share = -(-rows // count)
    if share * count != rows:
        block = jnp.pad(block, ((0, share * count - rows), (0, 0)))
    parts = lax.all_to_all(block.reshape(count, share, width), AXES, 0, 0)
    (mine,) = call(add_up_kernel, "add_up", [parts], [(parts.shape, F32)], limit=4 * 2**20)
    return lax.all_to_all(mine, AXES, 0, 0).reshape(count * share, width)[:rows]


def mm(left, right):
    return jnp.dot(left, right, precision=HIGH, preferred_element_type=F32)


def mm_tn(left, right):
    return lax.dot_general(
        left, right, (((0,), (0,)), ((), ())), precision=HIGH, preferred_element_type=F32
    )


def mm_nt(left, right):
    return lax.dot_general(
        left, right, (((1,), (1,)), ((), ())), precision=HIGH, preferred_element_type=F32
    )


def grid_of(shape, axis):
    return lax.broadcasted_iota(jnp.int32, shape, axis)


def identity(size):
    return jnp.where(grid_of((size, size), 0) == grid_of((size, size), 1), 1.0, 0.0).astype(F32)


def pivot_block(corner):
    size = corner.shape[0]
    columns = [jnp.broadcast_to(corner[:, t : t + 1], (size, LANES)) for t in range(size)]
    left = [[jnp.broadcast_to(columns[j][i : i + 1], (size, LANES)) for j in range(i + 1)] for i in range(size)]
    lower = [[None] * size for _ in range(size)]
    scales = []
    for j in range(size):
        scales.append(lax.rsqrt(left[j][j]))
        for i in range(j + 1, size):
            lower[i][j] = left[i][j] * scales[j]
        for i in range(j + 1, size):
            for k in range(j + 1, i + 1):
                left[i][k] = left[i][k] - lower[i][j] * lower[k][j]
    return lower, scales


def factor(gram):
    size = gram.shape[0]
    step = 8
    unit = identity(size)
    sides = [[m[r : r + step] for r in range(0, size, step)] for m in (gram, unit)]
    row = grid_of((step, size), 0)
    for p in range(size // step):
        base = p * step
        lower, scales = pivot_block(sides[0][p][:, base : base + step])
        leads = []
        for side in sides:
            rows = [jnp.broadcast_to(side[p][t : t + 1], (step, size)) for t in range(step)]
            for t in range(step):
                rows[t] = rows[t] * scales[t]
                for u in range(t + 1, step):
                    rows[u] = rows[u] - lower[u][t] * rows[t]
            strip = rows[0]
            for t in range(1, step):
                strip = jnp.where(row == t, rows[t], strip)
            side[p] = strip
            leads.append(rows)
        far = min(p + 1 + NEAR, size // step)
        for q in range(p + 1, far):
            strip = sides[0][q]
            columns = [jnp.broadcast_to(strip[:, base + t : base + t + 1], (step, size)) for t in range(step)]
            for t in range(step):
                share = columns[t] * scales[t]
                for u in range(t + 1, step):
                    columns[u] = columns[u] - share * lower[u][t]
                for side, lead in zip(sides, leads):
                    side[q] = side[q] - share * lead[t]
        if far * step < size:
            done = jnp.concatenate([side[p] for side in sides], 1)
            update = mm_tn(done[:, far * step : size], done)
            for q in range(far, size // step):
                at = (q - far) * step
                for k, side in enumerate(sides):
                    side[q] = side[q] - update[at : at + step, k * size : (k + 1) * size]
    upper = jnp.concatenate(sides[0], 0)
    upper = jnp.where(grid_of((size, size), 1) >= grid_of((size, size), 0), upper, 0.0)
    return upper, jnp.concatenate(sides[1], 0)


def rows_of(element, rows):
    return pl.ds(pl.multiple_of(element * rows, rows), rows)


def lanes_of(half, width):
    return pl.ds(pl.multiple_of(half * width, width), width)


def split(value):
    high = value.astype(BF16)
    return high, (value - high.astype(F32)).astype(BF16)


def take_traces(element, rows, picks_ref, field_ref, traces_ref):
    size = traces_ref.shape[1]
    rounded = field_ref[rows_of(element, rows), :].astype(BF16)
    picked = jnp.dot(picks_ref[...], rounded, preferred_element_type=F32).astype(BF16)
    for face in range(FACES):
        traces_ref[element * FACES + face] = picked[face * size : (face + 1) * size, :]


def pack(sends_ref, traces_ref, out_refs):
    for row, out_ref in enumerate(out_refs):
        for item in range(out_ref.shape[0]):
            out_ref[item] = traces_ref[sends_ref[0, row, item]]


def add_up_kernel(parts_ref, out_ref):
    out_ref[...] = jnp.broadcast_to(jnp.sum(parts_ref[...], axis=0, keepdims=True), out_ref.shape)


def start_gram_kernel(rhs_ref, damping_ref, out_ref):
    field = rhs_ref[...]
    width = field.shape[-1]
    gram = mm_tn(field, field)
    mass = jnp.sum(jnp.sum(damping_ref[...], axis=1, keepdims=True), axis=0, keepdims=True)
    corner = (grid_of(gram.shape, 0) == width - 1) & (grid_of(gram.shape, 1) == 0)
    out_ref[...] = jnp.where(corner, mass, gram)


def start_kernel(
    cells, gram_ref, rhs_ref, picks_ref, ssend_ref, csend_ref,
    field_ref, traces_ref, s0_ref, s1_ref, c0_ref, c1_ref, upper_ref, inverse_ref, center_ref,
):
    width = rhs_ref.shape[-1]
    half = width // 2
    count = traces_ref.shape[0] // FACES
    rows = rhs_ref.shape[0] // count
    raw = gram_ref[...]
    r, c = grid_of(raw.shape, 0), grid_of(raw.shape, 1)
    corner = (r == width - 1) & (c == 0)
    mass = raw[width - 1 : width, 0:1]
    raw = jnp.where(corner, raw[0:1, width - 1 : width], raw)
    center_ref[...] = jnp.broadcast_to(mass * (1.0 / cells), center_ref.shape)
    rr, ri = raw[:half, :half], raw[:half, half:]
    ir, ii = raw[half:, :half], raw[half:, half:]
    same, other = rr + ii, ir - ri
    gram = jnp.concatenate(
        [jnp.concatenate([same, other], 1), jnp.concatenate([-other, same], 1)], 0
    )
    upper, inverse = factor(gram)
    upper_ref[...] = upper
    inverse_ref[...] = inverse
    turn = inverse.T
    first = jnp.concatenate([turn[:half], -turn[half:]], 0)
    second = jnp.concatenate([turn[half:], turn[:half]], 0)
    wide = jnp.concatenate([first, second], 1)

    @pl.loop(0, count)
    def _(e):
        field_ref[rows_of(e, rows), :] = mm(rhs_ref[rows_of(e, rows), :], wide)
        take_traces(e, rows, picks_ref, field_ref, traces_ref)

    pack(ssend_ref, traces_ref, (s0_ref, s1_ref))
    pack(csend_ref, traces_ref, (c0_ref, c1_ref))


def next_kernel(
    level, red_ref, image_ref, *refs,
):
    basis = refs[: level + 1]
    picks_ref, ssend_ref, csend_ref = refs[level + 1 : level + 4]
    field_ref, traces_ref, s0_ref, s1_ref, c0_ref, c1_ref, upper_ref, inverse_ref = refs[level + 4 :]
    width = red_ref.shape[-1]
    blocks = [red_ref[j * width : (j + 1) * width, :] for j in range(level + 2)]
    coeffs = jnp.concatenate(blocks[:-1], 1)
    gram = blocks[-1] - mm_nt(coeffs, coeffs)
    upper, inverse = factor(gram)
    upper_ref[...] = upper
    inverse_ref[...] = inverse
    turn = inverse.T
    matrix = jnp.concatenate([turn, -mm_tn(coeffs, turn)], 0)
    count = traces_ref.shape[0] // FACES
    rows = field_ref.shape[0] // count

    @pl.loop(0, count)
    def _(e):
        at = rows_of(e, rows)
        for h in range(2):
            cut = slice(h * width, (h + 1) * width)
            parts = [ref[at, cut] for ref in (image_ref,) + basis]
            field_ref[at, cut] = mm(jnp.concatenate(parts, 1), matrix)
        take_traces(e, rows, picks_ref, field_ref, traces_ref)

    pack(ssend_ref, traces_ref, (s0_ref, s1_ref))
    pack(csend_ref, traces_ref, (c0_ref, c1_ref))


def turned(matrix):
    half = matrix.shape[0] // 2
    return jnp.concatenate([-matrix[half:], matrix[:half]], 0)


def inner_kernel(
    omega_ref, center_ref, damping_ref, diag_ref, field_ref, upper_ref, inverse_ref, *refs,
):
    part_ref, shift_ref, chain_out, unchain_out = refs[-4:]
    chain_refs = refs[:-4]
    chain, unchain = upper_ref[...], inverse_ref[...].T
    if chain_refs:
        chain = mm(chain, chain_refs[0][...])
        unchain = mm(chain_refs[1][...], unchain)
    chain_out[...] = chain
    unchain_out[...] = unchain
    omega = omega_ref[0]
    center = center_ref[0:1, 0:1]
    twist = omega * mm(chain, turned(unchain))
    shift_ref[...] = (twist + center * identity(twist.shape[0])).T
    width = twist.shape[0]
    rows = diag_ref.shape[1]

    @pl.loop(0, diag_ref.shape[0])
    def _(e):
        at = rows_of(e, rows)
        re, im = field_ref[at, :width], field_ref[at, width:]
        local = jnp.dot(diag_ref[e], field_ref[at, :].astype(BF16), preferred_element_type=F32)
        scale = jnp.swapaxes(damping_ref[pl.ds(e, 1), :] - center, 0, 1)
        part_ref[at, :width] = local[:, :width] + scale * re - omega * im - mm(re, twist)
        part_ref[at, width:] = local[:, width:] + scale * im + omega * re - mm(im, twist)


def square_kernel(
    sums0_ref, sums1_ref, shift0_ref, shift1_ref, shift2_ref, s0_ref, i1_ref, i2_ref, pack_ref,
):
    width = s0_ref.shape[0]
    t00 = sums0_ref[:width, :] + shift0_ref[...]
    t01 = sums1_ref[:width, :]
    t11 = sums1_ref[width : 2 * width, :] + shift1_ref[...]
    n1 = -mm(i1_ref[...], t00)
    n2 = -mm(i2_ref[...], t01 + mm(t11, n1))
    gram = identity(width) + mm_tn(n1, n1) + mm_tn(n2, n2)
    _, inverse = factor(gram)
    turn = inverse.T
    items = (turn, mm(n1, turn), mm(n2, turn), mm(inverse, s0_ref[...]), i1_ref[...], i2_ref[...])
    for at, item in enumerate(items + (mm_tn(i1_ref[...], t11.T), shift2_ref[...])):
        pack_ref[at] = item


def outer_kernel(level, list_ref, traces_ref, prev_ref, next_ref, cprev_ref, cnext_ref,
                 face_ref, part_ref, *refs):
    basis = refs[: level + 1]
    image_ref, out_ref, table, nearby = refs[level + 1 :]
    own = traces_ref.shape[0]
    size = traces_ref.shape[1]
    at = 0
    for ref in (traces_ref, prev_ref, next_ref, cprev_ref, cnext_ref):
        table[at : at + ref.shape[0]] = ref[...]
        at += ref.shape[0]
    table[at] = jnp.zeros(table.shape[1:], table.dtype)
    count, rows = face_ref.shape[:2]
    width = part_ref.shape[-1] // 2

    @pl.loop(0, count)
    def _(e):
        for f in range(FACES):
            nearby[f * size : (f + 1) * size, :] = table[list_ref[e, f]]
        coupled = jnp.dot(face_ref[e], nearby[...], preferred_element_type=F32)
        image_ref[rows_of(e, rows), :] = part_ref[rows_of(e, rows), :] + coupled

    out_ref[...] = jnp.zeros_like(out_ref)
    piece = 2 * width if (count * rows) % (2 * width) == 0 else rows

    @pl.loop(0, count * rows // piece)
    def _(i):
        @pl.loop(0, 2)
        def _(h):
            at = (rows_of(i, piece), lanes_of(h, width))
            parts = [split(ref[at]) for ref in basis + (image_ref,)]
            left = jnp.concatenate(parts[-1], 1)
            right = jnp.concatenate([jnp.concatenate([p[k] for p in parts], 1) for k in range(2)], 0)
            term = lax.dot_general(
                jnp.concatenate([left, left], 0),
                right,
                (((0,), (0,)), ((), ())),
                preferred_element_type=F32,
            )
            term = term[:width] + term[width:]
            for j in range(level + 2):
                out_ref[j * width : (j + 1) * width, :] += term[:, j * width : (j + 1) * width]


def final_kernel(
    red_ref, image_ref, v0_ref, v1_ref, v2_ref, pack_ref, solution_ref, residual_ref,
    fields, small, solved, left_over, in_sems, out_sems,
):
    load = pltpu.make_async_copy(pack_ref, small, in_sems.at[4])
    load.start()
    loads = [
        pltpu.make_async_copy(ref, fields.at[j], in_sems.at[j])
        for j, ref in enumerate((v0_ref, v1_ref, v2_ref, image_ref))
    ]
    for copy in loads:
        copy.start()
    width = red_ref.shape[-1]
    half = width // 2
    blocks = [red_ref[j * width : (j + 1) * width, :] for j in range(4)]
    coeffs = jnp.concatenate(blocks[:-1], 1)
    gram = blocks[-1] - mm_nt(coeffs, coeffs)
    load.wait()
    reach_in = small[0:3].reshape(3 * width, width)
    right, i1, i2, mixed, shift2 = [small[k] for k in range(3, 8)]
    shifted_coeffs = jnp.concatenate([coeffs[:, : 2 * width], coeffs[:, 2 * width :] + shift2], 1)
    reach = mm(shifted_coeffs, reach_in)
    goal = mm(reach, right)
    _, iq = factor(gram + mm_nt(reach, reach))
    y2 = mm_tn(iq, mm(iq, goal))
    z = mm(reach_in, right - mm_tn(reach, y2))
    z = [z[k * width : (k + 1) * width] for k in range(3)]
    hy = mm_tn(jnp.concatenate([coeffs, shift2], 1), y2)
    hy = [hy[k * width : (k + 1) * width] for k in range(4)]
    y1 = -mm_tn(i2, z[2] + hy[2] + hy[3])
    y0 = -mm_tn(i1, z[1] + hy[1]) - mm(mixed, y1)
    left = grid_of((width, width), 1) < half
    rows = []
    for y, w in ((y0, z[0] + hy[0]), (y1, z[1] + hy[1]), (y2, z[2] + hy[2]), (0.0 * y2, -y2)):
        rows.append(jnp.where(left, y, pltpu.roll(w, half, 1)))
    matrix = jnp.concatenate(rows, 0)
    count = out_sems.shape[1]
    size = solved.shape[0] // count
    lanes = grid_of((size, width), 1) < half
    for copy in loads:
        copy.wait()

    def copies(e):
        at = rows_of(e, size)
        return [
            pltpu.make_async_copy(solved.at[at], solution_ref.at[at], out_sems.at[0, e]),
            pltpu.make_async_copy(left_over.at[at], residual_ref.at[at], out_sems.at[1, e]),
        ]

    @pl.loop(0, count)
    def _(e):
        at = rows_of(e, size)

        cuts = [slice(h * width, (h + 1) * width) for h in range(2)]
        first, second = [
            mm(jnp.concatenate([fields[j, at, cut] for j in range(4)], 1), matrix) for cut in cuts
        ]
        solved[at, :] = jnp.where(lanes, first, pltpu.roll(second, half, 1))
        left_over[at, :] = jnp.where(lanes, pltpu.roll(first, half, 1), second)
        for copy in copies(e):
            copy.start()

    for e in range(count):
        for copy in copies(e):
            copy.wait()


def face_rows():
    grid = np.arange(NVAR * NP * NP * NP).reshape(NVAR, NP, NP, NP)
    faces = [
        grid[:, 0],
        grid[:, NP - 1],
        grid[:, :, 0],
        grid[:, :, NP - 1],
        grid[:, :, :, 0],
        grid[:, :, :, NP - 1],
    ]
    return np.concatenate([item.reshape(-1) for item in faces]).astype(np.int32)


VM = pl.BlockSpec(memory_space=pltpu.VMEM)
SM = pl.BlockSpec(memory_space=pltpu.SMEM)
AN = pl.BlockSpec(memory_space=pl.ANY)


def call(
    kernel, name, args, outs, scratch=(), scalars=(), flops=0, limit=VMEM_LIMIT, apart=(), out_apart=()
):
    moved = sum(a.size * a.dtype.itemsize for a in args)
    return pl.pallas_call(
        kernel,
        name=name,
        out_shape=[jax.ShapeDtypeStruct(shape, dtype) for shape, dtype in outs],
        in_specs=[SM if i in scalars else AN if i in apart else VM for i in range(len(args))],
        out_specs=[AN if i in out_apart else VM for i in range(len(outs))],
        scratch_shapes=list(scratch),
        compiler_params=pltpu.CompilerParams(vmem_limit_bytes=limit),
        cost_estimate=pl.CostEstimate(flops=flops, bytes_accessed=moved, transcendentals=0),
    )(*args)


def body(rhs, damping, omega, jac_diag, jac_face, face_list, stream_sends, cross_sends):
    count, rows, blocksize = rhs.shape
    columns = 2 * blocksize
    size = NVAR * NP * NP
    slots = count * FACES
    ss, sc = stream_sends.shape[-1], cross_sends.shape[-1]
    devices = lax.axis_size("stream") * lax.axis_size("cross")
    picks = np.zeros((FACES * size, rows), np.float32)
    picks[np.arange(FACES * size), face_rows()] = 1.0
    picks = jnp.asarray(picks, BF16)
    square = ((blocksize, blocksize), F32)
    field_out = ((count * rows, columns), F32)
    rhs = rhs.reshape(count * rows, blocksize)
    stage = [
        field_out,
        ((slots, size, columns), BF16),
        ((ss, size, columns), BF16),
        ((ss, size, columns), BF16),
        ((sc, size, columns), BF16),
        ((sc, size, columns), BF16),
        square,
        square,
    ]

    (gram,) = call(start_gram_kernel, "start_gram", [rhs, damping], [square])
    gram = total(gram)
    cells = float(devices * count * rows)
    field, traces, s0, s1, c0, c1, upper, inverse, center = call(
        functools.partial(start_kernel, cells),
        "start",
        [gram, rhs, picks, stream_sends, cross_sends],
        stage + [((8, blocksize), F32)],
        [],
        (3, 4),
    )
    basis, uppers, inverses, shifts, reduced = [field], [upper], [inverse], [], []
    chains = []
    for step in range(ITERS):
        from_prev = passed_along(s0, "stream", 1)
        from_next = passed_along(s1, "stream", -1)
        cross_prev = shifted(c0, "cross", 1)
        cross_next = shifted(c1, "cross", -1)
        part, shift, *chains = call(
            inner_kernel,
            "inner",
            [omega, center, damping, jac_diag, field, upper, inverse] + chains,
            [field_out, square, square, square],
            (),
            (0,),
            10**9,
        )
        shifts.append(shift)
        if step == ITERS - 1:
            (known,) = call(
                square_kernel,
                "square",
                reduced + shifts + [uppers[0], inverses[1], inverses[2]],
                [((8, blocksize, blocksize), F32)],
                (),
                (),
                10**9,
            )
        blocks = 2 if step == 0 else 4
        image, sums = call(
            functools.partial(outer_kernel, step),
            "outer",
            [face_list, traces, from_prev, from_next, cross_prev, cross_next, jac_face, part]
            + basis,
            [field_out, ((blocks * blocksize, blocksize), F32)],
            [
                pltpu.VMEM((slots + 2 * ss + 2 * sc + 1, size, columns), BF16),
                pltpu.VMEM((FACES * size, columns), BF16),
            ],
            (0,),
        )
        sums = total(sums)
        if step < ITERS - 1:
            reduced.append(sums)
            field, traces, s0, s1, c0, c1, upper, inverse = call(
                functools.partial(next_kernel, step),
                "next",
                [sums, image] + basis + [picks, stream_sends, cross_sends],
                stage,
                [],
                (step + 4, step + 5),
            )
            basis.append(field)
            uppers.append(upper)
            inverses.append(inverse)
    out = ((count * rows, blocksize), F32)
    results = call(
        final_kernel,
        "final",
        [sums, image] + basis + [known],
        [out, out],
        [
            pltpu.VMEM((4,) + field_out[0], F32),
            pltpu.VMEM((8, blocksize, blocksize), F32),
            pltpu.VMEM(*out),
            pltpu.VMEM(*out),
            pltpu.SemaphoreType.DMA((5,)),
            pltpu.SemaphoreType.DMA((2, count)),
        ],
        (),
        0,
        None,
        range(1, 6),
        (0, 1),
    )
    return tuple(item.reshape(count, rows, blocksize) for item in results)


def solution(mesh):
    in_specs = (
        P(("stream", "cross"), None, None),
        P(("stream", "cross"), None),
        P(),
        P(("stream", "cross"), None, None),
        P(("stream", "cross"), None, None),
        P(("stream", "cross"), None),
        P(("stream", "cross"), None, None),
        P(("stream", "cross"), None, None),
    )
    out_specs = (P(("stream", "cross"), None, None), P(("stream", "cross"), None, None))
    return jax.shard_map(body, mesh=mesh, in_specs=in_specs, out_specs=out_specs, check_vma=False)
```

```python
import functools
import jax
import jax.numpy as jnp
import numpy as np
from jax import lax
from jax.experimental import pallas as pl
from jax.experimental.pallas import tpu as pltpu
from jax.sharding import PartitionSpec as P

NP = 4
NVAR = 5
ITERS = 3
FACES = 6
AXES = ("stream", "cross")
HIGH = lax.Precision.HIGHEST
F32 = jnp.float32
BF16 = jnp.bfloat16
LANES = 128
NEAR = 4
VMEM_LIMIT = 20 * 2**20


def passed_along(value, axis, steps):
    count = lax.axis_size(axis)
    first, last = (max(0, -steps), min(count, count - steps))
    return lax.ppermute(value, axis, [(source, source + steps) for source in range(first, last)])


def shifted(block, axis, distance):
    devices = range(lax.axis_size(axis))
    route = [((i - distance) % len(devices), i) for i in devices]
    return lax.ppermute(block, axis, route)


def total(block):
    count = lax.axis_size(AXES[0]) * lax.axis_size(AXES[1])
    if block.ndim == 3:
        return exchange(block)
    rows, width = block.shape
    share = -(-rows // count)
    if share * count != rows:
        block = jnp.pad(block, ((0, share * count - rows), (0, 0)))
    return exchange(block.reshape(count, share, width)).reshape(count * share, width)[:rows]


def exchange(shares):
    parts = lax.all_to_all(shares, AXES, 0, 0)
    (mine,) = call(add_up_kernel, "add_up", [parts], [(parts.shape, F32)], limit=4 * 2**20)
    return lax.all_to_all(mine, AXES, 0, 0)


def mm(left, right):
    return jnp.dot(left, right, precision=HIGH, preferred_element_type=F32)


def mm_tn(left, right):
    return lax.dot_general(
        left, right, (((0,), (0,)), ((), ())), precision=HIGH, preferred_element_type=F32
    )


def mm_nt(left, right):
    return lax.dot_general(
        left, right, (((1,), (1,)), ((), ())), precision=HIGH, preferred_element_type=F32
    )


def grid_of(shape, axis):
    return lax.broadcasted_iota(jnp.int32, shape, axis)


def identity(size):
    return jnp.where(grid_of((size, size), 0) == grid_of((size, size), 1), 1.0, 0.0).astype(F32)


def pivot_block(corner):
    size = corner.shape[0]
    columns = [jnp.broadcast_to(corner[:, t : t + 1], (size, LANES)) for t in range(size)]
    left = [[jnp.broadcast_to(columns[j][i : i + 1], (size, LANES)) for j in range(i + 1)] for i in range(size)]
    lower = [[None] * size for _ in range(size)]
    scales = []
    for j in range(size):
        scales.append(lax.rsqrt(left[j][j]))
        for i in range(j + 1, size):
            lower[i][j] = left[i][j] * scales[j]
        for i in range(j + 1, size):
            for k in range(j + 1, i + 1):
                left[i][k] = left[i][k] - lower[i][j] * lower[k][j]
    return lower, scales


def factor(gram):
    size = gram.shape[0]
    step = 8
    unit = identity(size)
    sides = [[m[r : r + step] for r in range(0, size, step)] for m in (gram, unit)]
    row = grid_of((step, size), 0)
    for p in range(size // step):
        base = p * step
        lower, scales = pivot_block(sides[0][p][:, base : base + step])
        leads = []
        for side in sides:
            rows = [jnp.broadcast_to(side[p][t : t + 1], (step, size)) for t in range(step)]
            for t in range(step):
                rows[t] = rows[t] * scales[t]
                for u in range(t + 1, step):
                    rows[u] = rows[u] - lower[u][t] * rows[t]
            strip = rows[0]
            for t in range(1, step):
                strip = jnp.where(row == t, rows[t], strip)
            side[p] = strip
            leads.append(rows)
        far = min(p + 1 + NEAR, size // step)
        for q in range(p + 1, far):
            strip = sides[0][q]
            columns = [jnp.broadcast_to(strip[:, base + t : base + t + 1], (step, size)) for t in range(step)]
            for t in range(step):
                share = columns[t] * scales[t]
                for u in range(t + 1, step):
                    columns[u] = columns[u] - share * lower[u][t]
                for side, lead in zip(sides, leads):
                    side[q] = side[q] - share * lead[t]
        if far * step < size:
            done = jnp.concatenate([side[p] for side in sides], 1)
            update = mm_tn(done[:, far * step : size], done)
            for q in range(far, size // step):
                at = (q - far) * step
                for k, side in enumerate(sides):
                    side[q] = side[q] - update[at : at + step, k * size : (k + 1) * size]
    upper = jnp.concatenate(sides[0], 0)
    upper = jnp.where(grid_of((size, size), 1) >= grid_of((size, size), 0), upper, 0.0)
    return upper, jnp.concatenate(sides[1], 0)


def rows_of(element, rows):
    return pl.ds(pl.multiple_of(element * rows, rows), rows)


def lanes_of(half, width):
    return pl.ds(pl.multiple_of(half * width, width), width)


def blocks_of(ref, count):
    if len(ref.shape) == 2:
        size = ref.shape[-1]
        return [ref[j * size : (j + 1) * size, :] for j in range(count)]
    size = ref.shape[-1] // count
    wide = ref[...].reshape(size, count * size)
    return [wide[:, j * size : (j + 1) * size] for j in range(count)]


def split(value):
    high = value.astype(BF16)
    return high, (value - high.astype(F32)).astype(BF16)


def pieces_of(matrix):
    high, low = split(matrix)
    both = jnp.concatenate([high, low], 1)
    return jnp.concatenate([both, both], 0)


def mm_pieces(parts, weights):
    pairs = [split(part) for part in parts]
    left = jnp.concatenate([p[0] for p in pairs] + [p[1] for p in pairs], 1)
    out = jnp.dot(left, weights, preferred_element_type=F32)
    size = out.shape[1] // 2
    return out[:, :size] + out[:, size:]


def thirds_of(matrix):
    high, low = split(matrix)
    rest = (matrix - high.astype(F32) - low.astype(F32)).astype(BF16)
    both = jnp.concatenate([high, low], 1)
    last = jnp.concatenate([high, jnp.zeros_like(high)], 1)
    return jnp.concatenate([both, both, last], 0), rest


def mm_thirds(parts, weights):
    weights, rest = weights
    pairs = [split(part) for part in parts]
    thirds = [
        (part - p[0].astype(F32) - p[1].astype(F32)).astype(BF16) for part, p in zip(parts, pairs)
    ]
    high = [p[0] for p in pairs]
    left = jnp.concatenate(high + [p[1] for p in pairs] + thirds, 1)
    out = jnp.dot(left, weights, preferred_element_type=F32)
    tail = jnp.dot(jnp.concatenate(high, 1), rest, preferred_element_type=F32)
    size = out.shape[1] // 2
    return out[:, :size] + (out[:, size:] + tail)


def take_traces(element, rows, picks_ref, field_ref, traces_ref):
    size = traces_ref.shape[1]
    rounded = field_ref[rows_of(element, rows), :].astype(BF16)
    picked = jnp.dot(picks_ref[...], rounded, preferred_element_type=F32).astype(BF16)
    for face in range(FACES):
        traces_ref[element * FACES + face] = picked[face * size : (face + 1) * size, :]


def pack(sends_ref, traces_ref, out_refs):
    for row, out_ref in enumerate(out_refs):
        for item in range(out_ref.shape[0]):
            out_ref[item] = traces_ref[sends_ref[0, row, item]]


def add_up_kernel(parts_ref, out_ref):
    out_ref[...] = jnp.broadcast_to(jnp.sum(parts_ref[...], axis=0, keepdims=True), out_ref.shape)


def start_gram_kernel(rhs_ref, damping_ref, out_ref):
    field = rhs_ref[...]
    width = field.shape[-1]
    gram = mm_tn(field, field)
    mass = jnp.sum(jnp.sum(damping_ref[...], axis=1, keepdims=True), axis=0, keepdims=True)
    corner = (grid_of(gram.shape, 0) == width - 1) & (grid_of(gram.shape, 1) == 0)
    out_ref[...] = jnp.where(corner, mass, gram)


def start_kernel(
    cells, gram_ref, rhs_ref, picks_ref, ssend_ref, csend_ref,
    field_ref, traces_ref, s0_ref, s1_ref, c0_ref, c1_ref, upper_ref, inverse_ref, center_ref,
):
    width = rhs_ref.shape[-1]
    half = width // 2
    count = traces_ref.shape[0] // FACES
    rows = rhs_ref.shape[0] // count
    raw = gram_ref[...]
    r, c = grid_of(raw.shape, 0), grid_of(raw.shape, 1)
    corner = (r == width - 1) & (c == 0)
    mass = raw[width - 1 : width, 0:1]
    raw = jnp.where(corner, raw[0:1, width - 1 : width], raw)
    center_ref[...] = jnp.broadcast_to(mass * (1.0 / cells), center_ref.shape)
    rr, ri = raw[:half, :half], raw[:half, half:]
    ir, ii = raw[half:, :half], raw[half:, half:]
    same, other = rr + ii, ir - ri
    gram = jnp.concatenate(
        [jnp.concatenate([same, other], 1), jnp.concatenate([-other, same], 1)], 0
    )
    upper, inverse = factor(gram)
    upper_ref[...] = upper
    inverse_ref[...] = inverse
    turn = inverse.T
    first = jnp.concatenate([turn[:half], -turn[half:]], 0)
    second = jnp.concatenate([turn[half:], turn[:half]], 0)
    weights = thirds_of(first), thirds_of(second)

    @pl.loop(0, count)
    def _(e):
        field = [mm_thirds([rhs_ref[rows_of(e, rows), :]], item) for item in weights]
        field_ref[rows_of(e, rows), :] = jnp.concatenate(field, 1)
        take_traces(e, rows, picks_ref, field_ref, traces_ref)

    pack(ssend_ref, traces_ref, (s0_ref, s1_ref))
    pack(csend_ref, traces_ref, (c0_ref, c1_ref))


def next_kernel(
    level, red_ref, image_ref, *refs,
):
    basis = refs[: level + 1]
    picks_ref, ssend_ref, csend_ref = refs[level + 1 : level + 4]
    field_ref, traces_ref, s0_ref, s1_ref, c0_ref, c1_ref, upper_ref, inverse_ref = refs[level + 4 :]
    width = image_ref.shape[-1] // 2
    blocks = blocks_of(red_ref, level + 2)
    coeffs = jnp.concatenate(blocks[:-1], 1)
    gram = blocks[-1] - mm_nt(coeffs, coeffs)
    upper, inverse = factor(gram)
    upper_ref[...] = upper
    inverse_ref[...] = inverse
    turn = inverse.T
    weights = thirds_of(jnp.concatenate([turn, -mm_tn(coeffs, turn)], 0))
    count = traces_ref.shape[0] // FACES
    rows = field_ref.shape[0] // count

    @pl.loop(0, count)
    def _(e):
        at = rows_of(e, rows)
        for h in range(2):
            cut = slice(h * width, (h + 1) * width)
            parts = [ref[at, cut] for ref in (image_ref,) + basis]
            field_ref[at, cut] = mm_thirds(parts, weights)
        take_traces(e, rows, picks_ref, field_ref, traces_ref)

    pack(ssend_ref, traces_ref, (s0_ref, s1_ref))
    pack(csend_ref, traces_ref, (c0_ref, c1_ref))


def turned(matrix):
    half = matrix.shape[0] // 2
    return jnp.concatenate([-matrix[half:], matrix[:half]], 0)


def inner_kernel(
    omega_ref, center_ref, damping_ref, diag_ref, field_ref, upper_ref, inverse_ref, *refs,
):
    part_ref, shift_ref, chain_out, unchain_out = refs[-4:]
    chain_refs = refs[:-4]
    chain, unchain = upper_ref[...], inverse_ref[...].T
    if chain_refs:
        chain = mm(chain, chain_refs[0][...])
        unchain = mm(chain_refs[1][...], unchain)
    chain_out[...] = chain
    unchain_out[...] = unchain
    omega = omega_ref[0]
    center = center_ref[0:1, 0:1]
    twist = omega * mm(chain, turned(unchain))
    shift_ref[...] = (twist + center * identity(twist.shape[0])).T
    width = twist.shape[0]
    rows = diag_ref.shape[1]

    @pl.loop(0, diag_ref.shape[0])
    def _(e):
        at = rows_of(e, rows)
        re, im = field_ref[at, :width], field_ref[at, width:]
        local = jnp.dot(diag_ref[e], field_ref[at, :].astype(BF16), preferred_element_type=F32)
        scale = jnp.swapaxes(damping_ref[pl.ds(e, 1), :] - center, 0, 1)
        part_ref[at, :width] = local[:, :width] + scale * re - omega * im - mm(re, twist)
        part_ref[at, width:] = local[:, width:] + scale * im + omega * re - mm(im, twist)


def square_kernel(
    sums0_ref, sums1_ref, shift0_ref, shift1_ref, shift2_ref, s0_ref, i1_ref, i2_ref, pack_ref,
):
    width = s0_ref.shape[0]
    t00 = sums0_ref[:width, :] + shift0_ref[...]
    t01, t11, _ = blocks_of(sums1_ref, 3)
    t11 = t11 + shift1_ref[...]
    n1 = -mm(i1_ref[...], t00)
    n2 = -mm(i2_ref[...], t01 + mm(t11, n1))
    gram = identity(width) + mm_tn(n1, n1) + mm_tn(n2, n2)
    _, inverse = factor(gram)
    turn = inverse.T
    items = (turn, mm(n1, turn), mm(n2, turn), mm(inverse, s0_ref[...]), i1_ref[...], i2_ref[...])
    for at, item in enumerate(items + (mm_tn(i1_ref[...], t11.T), shift2_ref[...])):
        pack_ref[at] = item


def outer_kernel(level, list_ref, traces_ref, prev_ref, next_ref, cprev_ref, cnext_ref,
                 face_ref, part_ref, *refs):
    basis = refs[: level + 1]
    image_ref, out_ref, table, nearby, total_ref = refs[level + 1 :]
    own = traces_ref.shape[0]
    size = traces_ref.shape[1]
    at = 0
    for ref in (traces_ref, prev_ref, next_ref, cprev_ref, cnext_ref):
        table[at : at + ref.shape[0]] = ref[...]
        at += ref.shape[0]
    table[at] = jnp.zeros(table.shape[1:], table.dtype)
    count, rows = face_ref.shape[:2]
    width = part_ref.shape[-1] // 2

    @pl.loop(0, count)
    def _(e):
        for f in range(FACES):
            nearby[f * size : (f + 1) * size, :] = table[list_ref[e, f]]
        coupled = jnp.dot(face_ref[e], nearby[...], preferred_element_type=F32)
        image_ref[rows_of(e, rows), :] = part_ref[rows_of(e, rows), :] + coupled

    sums_ref = out_ref if len(out_ref.shape) == 2 else total_ref
    sums_ref[...] = jnp.zeros_like(sums_ref)
    piece = 2 * width if (count * rows) % (2 * width) == 0 else rows

    @pl.loop(0, count * rows // piece)
    def _(i):
        @pl.loop(0, 2)
        def _(h):
            at = (rows_of(i, piece), lanes_of(h, width))
            parts = [split(ref[at]) for ref in basis + (image_ref,)]
            left = jnp.concatenate(parts[-1], 1)
            right = jnp.concatenate([jnp.concatenate([p[k] for p in parts], 1) for k in range(2)], 0)
            term = lax.dot_general(
                jnp.concatenate([left, left], 0),
                right,
                (((0,), (0,)), ((), ())),
                preferred_element_type=F32,
            )
            term = term[:width] + term[width:]
            if len(out_ref.shape) == 3:
                sums_ref[...] += term
            else:
                for j in range(level + 2):
                    sums_ref[j * width : (j + 1) * width, :] += term[:, j * width : (j + 1) * width]

    if len(out_ref.shape) == 3:
        out_ref[...] = sums_ref[...].reshape(out_ref.shape)


def final_kernel(
    red_ref, image_ref, v0_ref, v1_ref, v2_ref, pack_ref, solution_ref, residual_ref,
    fields, small, solved, left_over, in_sems, out_sems,
):
    load = pltpu.make_async_copy(pack_ref, small, in_sems.at[4])
    load.start()
    loads = [
        pltpu.make_async_copy(ref, fields.at[j], in_sems.at[j])
        for j, ref in enumerate((v0_ref, v1_ref, v2_ref, image_ref))
    ]
    for copy in loads:
        copy.start()
    width = red_ref.shape[-1]
    half = width // 2
    blocks = [red_ref[j * width : (j + 1) * width, :] for j in range(4)]
    coeffs = jnp.concatenate(blocks[:-1], 1)
    gram = blocks[-1] - mm_nt(coeffs, coeffs)
    load.wait()
    reach_in = small[0:3].reshape(3 * width, width)
    right, i1, i2, mixed, shift2 = [small[k] for k in range(3, 8)]
    shifted_coeffs = jnp.concatenate([coeffs[:, : 2 * width], coeffs[:, 2 * width :] + shift2], 1)
    reach = mm(shifted_coeffs, reach_in)
    goal = mm(reach, right)
    _, iq = factor(gram + mm_nt(reach, reach))
    y2 = mm_tn(iq, mm(iq, goal))
    z = mm(reach_in, right - mm_tn(reach, y2))
    z = [z[k * width : (k + 1) * width] for k in range(3)]
    hy = mm_tn(jnp.concatenate([coeffs, shift2], 1), y2)
    hy = [hy[k * width : (k + 1) * width] for k in range(4)]
    y1 = -mm_tn(i2, z[2] + hy[2] + hy[3])
    y0 = -mm_tn(i1, z[1] + hy[1]) - mm(mixed, y1)
    left = grid_of((width, width), 1) < half
    rows = []
    for y, w in ((y0, z[0] + hy[0]), (y1, z[1] + hy[1]), (y2, z[2] + hy[2]), (0.0 * y2, -y2)):
        rows.append(jnp.where(left, y, pltpu.roll(w, half, 1)))
    weights = pieces_of(jnp.concatenate(rows, 0))
    count = out_sems.shape[1]
    size = solved.shape[0] // count
    lanes = grid_of((size, width), 1) < half
    for copy in loads:
        copy.wait()

    def copies(e):
        at = rows_of(e, size)
        return [
            pltpu.make_async_copy(solved.at[at], solution_ref.at[at], out_sems.at[0, e]),
            pltpu.make_async_copy(left_over.at[at], residual_ref.at[at], out_sems.at[1, e]),
        ]

    @pl.loop(0, count)
    def _(e):
        at = rows_of(e, size)

        cuts = [slice(h * width, (h + 1) * width) for h in range(2)]
        first, second = [mm_pieces([fields[j, at, cut] for j in range(4)], weights) for cut in cuts]
        solved[at, :] = jnp.where(lanes, first, pltpu.roll(second, half, 1))
        left_over[at, :] = jnp.where(lanes, pltpu.roll(first, half, 1), second)
        for copy in copies(e):
            copy.start()

    for e in range(count):
        for copy in copies(e):
            copy.wait()


def face_rows():
    grid = np.arange(NVAR * NP * NP * NP).reshape(NVAR, NP, NP, NP)
    faces = [
        grid[:, 0],
        grid[:, NP - 1],
        grid[:, :, 0],
        grid[:, :, NP - 1],
        grid[:, :, :, 0],
        grid[:, :, :, NP - 1],
    ]
    return np.concatenate([item.reshape(-1) for item in faces]).astype(np.int32)


VM = pl.BlockSpec(memory_space=pltpu.VMEM)
SM = pl.BlockSpec(memory_space=pltpu.SMEM)
AN = pl.BlockSpec(memory_space=pl.ANY)


def call(
    kernel, name, args, outs, scratch=(), scalars=(), flops=0, limit=VMEM_LIMIT, apart=(), out_apart=()
):
    moved = sum(a.size * a.dtype.itemsize for a in args)
    return pl.pallas_call(
        kernel,
        name=name,
        out_shape=[jax.ShapeDtypeStruct(shape, dtype) for shape, dtype in outs],
        in_specs=[SM if i in scalars else AN if i in apart else VM for i in range(len(args))],
        out_specs=[AN if i in out_apart else VM for i in range(len(outs))],
        scratch_shapes=list(scratch),
        compiler_params=pltpu.CompilerParams(vmem_limit_bytes=limit),
        cost_estimate=pl.CostEstimate(flops=flops, bytes_accessed=moved, transcendentals=0),
    )(*args)


def body(rhs, damping, omega, jac_diag, jac_face, face_list, stream_sends, cross_sends):
    count, rows, blocksize = rhs.shape
    columns = 2 * blocksize
    size = NVAR * NP * NP
    slots = count * FACES
    ss, sc = stream_sends.shape[-1], cross_sends.shape[-1]
    devices = lax.axis_size("stream") * lax.axis_size("cross")
    picks = np.zeros((FACES * size, rows), np.float32)
    picks[np.arange(FACES * size), face_rows()] = 1.0
    picks = jnp.asarray(picks, BF16)
    square = ((blocksize, blocksize), F32)
    field_out = ((count * rows, columns), F32)
    rhs = rhs.reshape(count * rows, blocksize)
    stage = [
        field_out,
        ((slots, size, columns), BF16),
        ((ss, size, columns), BF16),
        ((ss, size, columns), BF16),
        ((sc, size, columns), BF16),
        ((sc, size, columns), BF16),
        square,
        square,
    ]

    (gram,) = call(start_gram_kernel, "start_gram", [rhs, damping], [square])
    gram = total(gram)
    cells = float(devices * count * rows)
    field, traces, s0, s1, c0, c1, upper, inverse, center = call(
        functools.partial(start_kernel, cells),
        "start",
        [gram, rhs, picks, stream_sends, cross_sends],
        stage + [((8, blocksize), F32)],
        [],
        (3, 4),
    )
    basis, uppers, inverses, shifts, reduced = [field], [upper], [inverse], [], []
    chains = []
    for step in range(ITERS):
        from_prev = passed_along(s0, "stream", 1)
        from_next = passed_along(s1, "stream", -1)
        cross_prev = shifted(c0, "cross", 1)
        cross_next = shifted(c1, "cross", -1)
        part, shift, *chains = call(
            inner_kernel,
            "inner",
            [omega, center, damping, jac_diag, field, upper, inverse] + chains,
            [field_out, square, square, square],
            (),
            (0,),
            10**9,
        )
        shifts.append(shift)
        if step == ITERS - 1:
            (known,) = call(
                square_kernel,
                "square",
                reduced + shifts + [uppers[0], inverses[1], inverses[2]],
                [((8, blocksize, blocksize), F32)],
                (),
                (),
                10**9,
            )
        wide = (blocksize, (step + 2) * blocksize)
        sums_out = ((step + 2) * blocksize, blocksize)
        if step == 1:
            sums_out = (4 * blocksize, blocksize)
            if blocksize % devices == 0:
                sums_out = (devices, blocksize // devices, wide[1])
        image, sums = call(
            functools.partial(outer_kernel, step),
            "outer",
            [face_list, traces, from_prev, from_next, cross_prev, cross_next, jac_face, part]
            + basis,
            [field_out, (sums_out, F32)],
            [
                pltpu.VMEM((slots + 2 * ss + 2 * sc + 1, size, columns), BF16),
                pltpu.VMEM((FACES * size, columns), BF16),
                pltpu.VMEM(wide, F32),
            ],
            (0,),
        )
        sums = total(sums)
        if step < ITERS - 1:
            reduced.append(sums)
            field, traces, s0, s1, c0, c1, upper, inverse = call(
                functools.partial(next_kernel, step),
                "next",
                [sums, image] + basis + [picks, stream_sends, cross_sends],
                stage,
                [],
                (step + 4, step + 5),
            )
            basis.append(field)
            uppers.append(upper)
            inverses.append(inverse)
    out = ((count * rows, blocksize), F32)
    results = call(
        final_kernel,
        "final",
        [sums, image] + basis + [known],
        [out, out],
        [
            pltpu.VMEM((4,) + field_out[0], F32),
            pltpu.VMEM((8, blocksize, blocksize), F32),
            pltpu.VMEM(*out),
            pltpu.VMEM(*out),
            pltpu.SemaphoreType.DMA((5,)),
            pltpu.SemaphoreType.DMA((2, count)),
        ],
        (),
        0,
        None,
        range(1, 6),
        (0, 1),
    )
    return tuple(item.reshape(count, rows, blocksize) for item in results)


def solution(mesh):
    in_specs = (
        P(("stream", "cross"), None, None),
        P(("stream", "cross"), None),
        P(),
        P(("stream", "cross"), None, None),
        P(("stream", "cross"), None, None),
        P(("stream", "cross"), None),
        P(("stream", "cross"), None, None),
        P(("stream", "cross"), None, None),
    )
    out_specs = (P(("stream", "cross"), None, None), P(("stream", "cross"), None, None))
    return jax.shard_map(body, mesh=mesh, in_specs=in_specs, out_specs=out_specs, check_vma=False)
```

```python
import functools
import jax
import jax.numpy as jnp
import numpy as np
from jax import lax
from jax.experimental import pallas as pl
from jax.experimental.pallas import tpu as pltpu
from jax.sharding import PartitionSpec as P

NP = 4
NVAR = 5
ITERS = 3
FACES = 6
AXES = ("stream", "cross")
HIGH = lax.Precision.HIGHEST
F32 = jnp.float32
BF16 = jnp.bfloat16
LANES = 128
NEAR = 4
VMEM_LIMIT = 20 * 2**20


def passed_along(value, axis, steps):
    count = lax.axis_size(axis)
    first, last = (max(0, -steps), min(count, count - steps))
    return lax.ppermute(value, axis, [(source, source + steps) for source in range(first, last)])


def shifted(block, axis, distance):
    devices = range(lax.axis_size(axis))
    route = [((i - distance) % len(devices), i) for i in devices]
    return lax.ppermute(block, axis, route)


def total(block):
    count = lax.axis_size(AXES[0]) * lax.axis_size(AXES[1])
    if block.ndim == 3:
        return exchange(block)
    rows, width = block.shape
    share = -(-rows // count)
    if share * count != rows:
        block = jnp.pad(block, ((0, share * count - rows), (0, 0)))
    return exchange(block.reshape(count, share, width)).reshape(count * share, width)[:rows]


def exchange(shares):
    parts = lax.all_to_all(shares, AXES, 0, 0)
    (mine,) = call(add_up_kernel, "add_up", [parts], [(parts.shape, F32)], limit=4 * 2**20)
    return lax.all_to_all(mine, AXES, 0, 0)


def mm(left, right):
    return jnp.dot(left, right, precision=HIGH, preferred_element_type=F32)


def mm_tn(left, right):
    return lax.dot_general(
        left, right, (((0,), (0,)), ((), ())), precision=HIGH, preferred_element_type=F32
    )


def mm_nt(left, right):
    return lax.dot_general(
        left, right, (((1,), (1,)), ((), ())), precision=HIGH, preferred_element_type=F32
    )


def grid_of(shape, axis):
    return lax.broadcasted_iota(jnp.int32, shape, axis)


def identity(size):
    return jnp.where(grid_of((size, size), 0) == grid_of((size, size), 1), 1.0, 0.0).astype(F32)


def pivot_block(corner):
    size = corner.shape[0]
    columns = [jnp.broadcast_to(corner[:, t : t + 1], (size, LANES)) for t in range(size)]
    left = [[jnp.broadcast_to(columns[j][i : i + 1], (size, LANES)) for j in range(i + 1)] for i in range(size)]
    lower = [[None] * size for _ in range(size)]
    scales = []
    for j in range(size):
        scales.append(lax.rsqrt(left[j][j]))
        for i in range(j + 1, size):
            lower[i][j] = left[i][j] * scales[j]
        for i in range(j + 1, size):
            for k in range(j + 1, i + 1):
                left[i][k] = left[i][k] - lower[i][j] * lower[k][j]
    return lower, scales


def factor(gram):
    size = gram.shape[0]
    step = 8
    unit = identity(size)
    sides = [[m[r : r + step] for r in range(0, size, step)] for m in (gram, unit)]
    row = grid_of((step, size), 0)
    for p in range(size // step):
        base = p * step
        lower, scales = pivot_block(sides[0][p][:, base : base + step])
        leads = []
        for side in sides:
            rows = [jnp.broadcast_to(side[p][t : t + 1], (step, size)) for t in range(step)]
            for t in range(step):
                rows[t] = rows[t] * scales[t]
                for u in range(t + 1, step):
                    rows[u] = rows[u] - lower[u][t] * rows[t]
            strip = rows[0]
            for t in range(1, step):
                strip = jnp.where(row == t, rows[t], strip)
            side[p] = strip
            leads.append(rows)
        far = min(p + 1 + NEAR, size // step)
        for q in range(p + 1, far):
            strip = sides[0][q]
            columns = [jnp.broadcast_to(strip[:, base + t : base + t + 1], (step, size)) for t in range(step)]
            for t in range(step):
                share = columns[t] * scales[t]
                for u in range(t + 1, step):
                    columns[u] = columns[u] - share * lower[u][t]
                for side, lead in zip(sides, leads):
                    side[q] = side[q] - share * lead[t]
        if far * step < size:
            done = jnp.concatenate([side[p] for side in sides], 1)
            update = mm_tn(done[:, far * step : size], done)
            for q in range(far, size // step):
                at = (q - far) * step
                for k, side in enumerate(sides):
                    side[q] = side[q] - update[at : at + step, k * size : (k + 1) * size]
    upper = jnp.concatenate(sides[0], 0)
    upper = jnp.where(grid_of((size, size), 1) >= grid_of((size, size), 0), upper, 0.0)
    return upper, jnp.concatenate(sides[1], 0)


def rows_of(element, rows):
    return pl.ds(pl.multiple_of(element * rows, rows), rows)


def lanes_of(half, width):
    return pl.ds(pl.multiple_of(half * width, width), width)


def blocks_of(ref, count):
    if len(ref.shape) == 2:
        size = ref.shape[-1]
        return [ref[j * size : (j + 1) * size, :] for j in range(count)]
    size = ref.shape[-1] // count
    wide = ref[...].reshape(size, count * size)
    return [wide[:, j * size : (j + 1) * size] for j in range(count)]


def split(value):
    high = value.astype(BF16)
    return high, (value - high.astype(F32)).astype(BF16)


def pieces_of(matrix):
    high, low = split(matrix)
    both = jnp.concatenate([high, low], 1)
    return jnp.concatenate([both, both], 0)


def mm_pieces(parts, weights):
    pairs = [split(part) for part in parts]
    left = jnp.concatenate([p[0] for p in pairs] + [p[1] for p in pairs], 1)
    out = jnp.dot(left, weights, preferred_element_type=F32)
    size = out.shape[1] // 2
    return out[:, :size] + out[:, size:]


def thirds_of(matrix):
    high, low = split(matrix)
    rest = (matrix - high.astype(F32) - low.astype(F32)).astype(BF16)
    both = jnp.concatenate([high, low], 1)
    last = jnp.concatenate([high, jnp.zeros_like(high)], 1)
    return jnp.concatenate([both, both, last], 0), rest


def mm_thirds(parts, weights):
    weights, rest = weights
    pairs = [split(part) for part in parts]
    thirds = [
        (part - p[0].astype(F32) - p[1].astype(F32)).astype(BF16) for part, p in zip(parts, pairs)
    ]
    high = [p[0] for p in pairs]
    left = jnp.concatenate(high + [p[1] for p in pairs] + thirds, 1)
    out = jnp.dot(left, weights, preferred_element_type=F32)
    tail = jnp.dot(jnp.concatenate(high, 1), rest, preferred_element_type=F32)
    size = out.shape[1] // 2
    return out[:, :size] + (out[:, size:] + tail)


def take_traces(element, rows, picks_ref, field_ref, traces_ref):
    size = traces_ref.shape[1]
    rounded = field_ref[rows_of(element, rows), :].astype(BF16)
    picked = jnp.dot(picks_ref[...], rounded, preferred_element_type=F32).astype(BF16)
    for face in range(FACES):
        traces_ref[element * FACES + face] = picked[face * size : (face + 1) * size, :]


def pack(sends_ref, traces_ref, out_refs):
    for row, out_ref in enumerate(out_refs):
        for item in range(out_ref.shape[0]):
            out_ref[item] = traces_ref[sends_ref[0, row, item]]


def add_up_kernel(parts_ref, out_ref):
    out_ref[...] = jnp.broadcast_to(jnp.sum(parts_ref[...], axis=0, keepdims=True), out_ref.shape)


def start_gram_kernel(rhs_ref, damping_ref, out_ref):
    width = rhs_ref.shape[-1]
    both = jnp.concatenate(split(rhs_ref[...]), 1)
    gram = lax.dot_general(both, both, (((0,), (0,)), ((), ())), preferred_element_type=F32)
    gram = gram[:width] + gram[width:]
    gram = gram[:, :width] + gram[:, width:]
    mass = jnp.sum(jnp.sum(damping_ref[...], axis=1, keepdims=True), axis=0, keepdims=True)
    corner = (grid_of(gram.shape, 0) == width - 1) & (grid_of(gram.shape, 1) == 0)
    out_ref[...] = jnp.where(corner, mass, gram)


def start_kernel(
    cells, gram_ref, rhs_ref, picks_ref, ssend_ref, csend_ref,
    field_ref, traces_ref, s0_ref, s1_ref, c0_ref, c1_ref, upper_ref, inverse_ref, center_ref,
):
    width = rhs_ref.shape[-1]
    half = width // 2
    count = traces_ref.shape[0] // FACES
    rows = rhs_ref.shape[0] // count
    raw = gram_ref[...]
    r, c = grid_of(raw.shape, 0), grid_of(raw.shape, 1)
    corner = (r == width - 1) & (c == 0)
    mass = raw[width - 1 : width, 0:1]
    raw = jnp.where(corner, raw[0:1, width - 1 : width], raw)
    center_ref[...] = jnp.broadcast_to(mass * (1.0 / cells), center_ref.shape)
    rr, ri = raw[:half, :half], raw[:half, half:]
    ir, ii = raw[half:, :half], raw[half:, half:]
    same, other = rr + ii, ir - ri
    gram = jnp.concatenate(
        [jnp.concatenate([same, other], 1), jnp.concatenate([-other, same], 1)], 0
    )
    upper, inverse = factor(gram)
    upper_ref[...] = upper
    inverse_ref[...] = inverse
    turn = inverse.T
    first = jnp.concatenate([turn[:half], -turn[half:]], 0)
    second = jnp.concatenate([turn[half:], turn[:half]], 0)
    weights = thirds_of(first), thirds_of(second)

    @pl.loop(0, count)
    def _(e):
        field = [mm_thirds([rhs_ref[rows_of(e, rows), :]], item) for item in weights]
        field_ref[rows_of(e, rows), :] = jnp.concatenate(field, 1)
        take_traces(e, rows, picks_ref, field_ref, traces_ref)

    pack(ssend_ref, traces_ref, (s0_ref, s1_ref))
    pack(csend_ref, traces_ref, (c0_ref, c1_ref))


def next_kernel(
    level, red_ref, image_ref, *refs,
):
    basis = refs[: level + 1]
    picks_ref, ssend_ref, csend_ref = refs[level + 1 : level + 4]
    field_ref, traces_ref, s0_ref, s1_ref, c0_ref, c1_ref, upper_ref, inverse_ref = refs[level + 4 :]
    width = image_ref.shape[-1] // 2
    blocks = blocks_of(red_ref, level + 2)
    coeffs = jnp.concatenate(blocks[:-1], 1)
    gram = blocks[-1] - mm_nt(coeffs, coeffs)
    upper, inverse = factor(gram)
    upper_ref[...] = upper
    inverse_ref[...] = inverse
    turn = inverse.T
    weights = thirds_of(jnp.concatenate([turn, -mm_tn(coeffs, turn)], 0))
    count = traces_ref.shape[0] // FACES
    rows = field_ref.shape[0] // count

    @pl.loop(0, count)
    def _(e):
        at = rows_of(e, rows)
        for h in range(2):
            cut = slice(h * width, (h + 1) * width)
            parts = [ref[at, cut] for ref in (image_ref,) + basis]
            field_ref[at, cut] = mm_thirds(parts, weights)
        take_traces(e, rows, picks_ref, field_ref, traces_ref)

    pack(ssend_ref, traces_ref, (s0_ref, s1_ref))
    pack(csend_ref, traces_ref, (c0_ref, c1_ref))


def turned(matrix):
    half = matrix.shape[0] // 2
    return jnp.concatenate([-matrix[half:], matrix[:half]], 0)


def inner_kernel(
    omega_ref, center_ref, damping_ref, diag_ref, field_ref, upper_ref, inverse_ref, *refs,
):
    part_ref, shift_ref, chain_out, unchain_out = refs[-4:]
    chain_refs = refs[:-4]
    chain, unchain = upper_ref[...], inverse_ref[...].T
    if chain_refs:
        chain = mm(chain, chain_refs[0][...])
        unchain = mm(chain_refs[1][...], unchain)
    chain_out[...] = chain
    unchain_out[...] = unchain
    omega = omega_ref[0]
    center = center_ref[0:1, 0:1]
    twist = omega * mm(chain, turned(unchain))
    shift_ref[...] = (twist + center * identity(twist.shape[0])).T
    width = twist.shape[0]
    rows = diag_ref.shape[1]

    @pl.loop(0, diag_ref.shape[0])
    def _(e):
        at = rows_of(e, rows)
        re, im = field_ref[at, :width], field_ref[at, width:]
        local = jnp.dot(diag_ref[e], field_ref[at, :].astype(BF16), preferred_element_type=F32)
        scale = jnp.swapaxes(damping_ref[pl.ds(e, 1), :] - center, 0, 1)
        part_ref[at, :width] = local[:, :width] + scale * re - omega * im - mm(re, twist)
        part_ref[at, width:] = local[:, width:] + scale * im + omega * re - mm(im, twist)


def square_kernel(
    sums0_ref, sums1_ref, shift0_ref, shift1_ref, shift2_ref, s0_ref, i1_ref, i2_ref, pack_ref,
):
    width = s0_ref.shape[0]
    t00 = sums0_ref[:width, :] + shift0_ref[...]
    t01, t11, _ = blocks_of(sums1_ref, 3)
    t11 = t11 + shift1_ref[...]
    n1 = -mm(i1_ref[...], t00)
    n2 = -mm(i2_ref[...], t01 + mm(t11, n1))
    gram = identity(width) + mm_tn(n1, n1) + mm_tn(n2, n2)
    _, inverse = factor(gram)
    turn = inverse.T
    items = (turn, mm(n1, turn), mm(n2, turn), mm(inverse, s0_ref[...]), i1_ref[...], i2_ref[...])
    for at, item in enumerate(items + (mm_tn(i1_ref[...], t11.T), shift2_ref[...])):
        pack_ref[at] = item


def outer_kernel(level, list_ref, traces_ref, prev_ref, next_ref, cprev_ref, cnext_ref,
                 face_ref, part_ref, *refs):
    basis = refs[: level + 1]
    image_ref, out_ref, table, nearby, total_ref = refs[level + 1 :]
    own = traces_ref.shape[0]
    size = traces_ref.shape[1]
    at = 0
    for ref in (traces_ref, prev_ref, next_ref, cprev_ref, cnext_ref):
        table[at : at + ref.shape[0]] = ref[...]
        at += ref.shape[0]
    table[at] = jnp.zeros(table.shape[1:], table.dtype)
    count, rows = face_ref.shape[:2]
    width = part_ref.shape[-1] // 2

    @pl.loop(0, count)
    def _(e):
        for f in range(FACES):
            nearby[f * size : (f + 1) * size, :] = table[list_ref[e, f]]
        coupled = jnp.dot(face_ref[e], nearby[...], preferred_element_type=F32)
        image_ref[rows_of(e, rows), :] = part_ref[rows_of(e, rows), :] + coupled

    sums_ref = out_ref if len(out_ref.shape) == 2 else total_ref
    sums_ref[...] = jnp.zeros_like(sums_ref)
    piece = 2 * width if (count * rows) % (2 * width) == 0 else rows

    @pl.loop(0, count * rows // piece)
    def _(i):
        lefts, rights = [], []
        for h in range(2):
            at = (rows_of(i, piece), slice(h * width, (h + 1) * width))
            parts = [split(ref[at]) for ref in basis + (image_ref,)]
            lefts += [jnp.concatenate(parts[-1], 1)] * 2
            rights += [jnp.concatenate([p[k] for p in parts], 1) for k in range(2)]
        term = lax.dot_general(
            jnp.concatenate(lefts, 0),
            jnp.concatenate(rights, 0),
            (((0,), (0,)), ((), ())),
            preferred_element_type=F32,
        )
        term = term[:width] + term[width:]
        if len(out_ref.shape) == 3:
            sums_ref[...] += term
        else:
            for j in range(level + 2):
                sums_ref[j * width : (j + 1) * width, :] += term[:, j * width : (j + 1) * width]

    if len(out_ref.shape) == 3:
        out_ref[...] = sums_ref[...].reshape(out_ref.shape)


def final_kernel(
    red_ref, image_ref, v0_ref, v1_ref, v2_ref, pack_ref, solution_ref, residual_ref,
    fields, small, solved, left_over, in_sems, out_sems,
):
    load = pltpu.make_async_copy(pack_ref, small, in_sems.at[4])
    load.start()
    loads = [
        pltpu.make_async_copy(ref, fields.at[j], in_sems.at[j])
        for j, ref in enumerate((v0_ref, v1_ref, v2_ref, image_ref))
    ]
    for copy in loads:
        copy.start()
    width = red_ref.shape[-1]
    half = width // 2
    blocks = [red_ref[j * width : (j + 1) * width, :] for j in range(4)]
    coeffs = jnp.concatenate(blocks[:-1], 1)
    gram = blocks[-1] - mm_nt(coeffs, coeffs)
    load.wait()
    reach_in = small[0:3].reshape(3 * width, width)
    right, i1, i2, mixed, shift2 = [small[k] for k in range(3, 8)]
    shifted_coeffs = jnp.concatenate([coeffs[:, : 2 * width], coeffs[:, 2 * width :] + shift2], 1)
    reach = mm(shifted_coeffs, reach_in)
    goal = mm(reach, right)
    _, iq = factor(gram + mm_nt(reach, reach))
    y2 = mm_tn(iq, mm(iq, goal))
    z = mm(reach_in, right - mm_tn(reach, y2))
    z = [z[k * width : (k + 1) * width] for k in range(3)]
    hy = mm_tn(jnp.concatenate([coeffs, shift2], 1), y2)
    hy = [hy[k * width : (k + 1) * width] for k in range(4)]
    y1 = -mm_tn(i2, z[2] + hy[2] + hy[3])
    y0 = -mm_tn(i1, z[1] + hy[1]) - mm(mixed, y1)
    left = grid_of((width, width), 1) < half
    rows = []
    for y, w in ((y0, z[0] + hy[0]), (y1, z[1] + hy[1]), (y2, z[2] + hy[2]), (0.0 * y2, -y2)):
        rows.append(jnp.where(left, y, pltpu.roll(w, half, 1)))
    weights = pieces_of(jnp.concatenate(rows, 0))
    count = out_sems.shape[1]
    size = solved.shape[0] // count
    lanes = grid_of((size, width), 1) < half
    for copy in loads:
        copy.wait()

    def copies(e):
        at = rows_of(e, size)
        return [
            pltpu.make_async_copy(solved.at[at], solution_ref.at[at], out_sems.at[0, e]),
            pltpu.make_async_copy(left_over.at[at], residual_ref.at[at], out_sems.at[1, e]),
        ]

    @pl.loop(0, count)
    def _(e):
        at = rows_of(e, size)

        cuts = [slice(h * width, (h + 1) * width) for h in range(2)]
        first, second = [mm_pieces([fields[j, at, cut] for j in range(4)], weights) for cut in cuts]
        solved[at, :] = jnp.where(lanes, first, pltpu.roll(second, half, 1))
        left_over[at, :] = jnp.where(lanes, pltpu.roll(first, half, 1), second)
        for copy in copies(e):
            copy.start()

    for e in range(count):
        for copy in copies(e):
            copy.wait()


def face_rows():
    grid = np.arange(NVAR * NP * NP * NP).reshape(NVAR, NP, NP, NP)
    faces = [
        grid[:, 0],
        grid[:, NP - 1],
        grid[:, :, 0],
        grid[:, :, NP - 1],
        grid[:, :, :, 0],
        grid[:, :, :, NP - 1],
    ]
    return np.concatenate([item.reshape(-1) for item in faces]).astype(np.int32)


VM = pl.BlockSpec(memory_space=pltpu.VMEM)
SM = pl.BlockSpec(memory_space=pltpu.SMEM)
AN = pl.BlockSpec(memory_space=pl.ANY)


def call(
    kernel, name, args, outs, scratch=(), scalars=(), flops=0, limit=VMEM_LIMIT, apart=(), out_apart=()
):
    moved = sum(a.size * a.dtype.itemsize for a in args)
    return pl.pallas_call(
        kernel,
        name=name,
        out_shape=[jax.ShapeDtypeStruct(shape, dtype) for shape, dtype in outs],
        in_specs=[SM if i in scalars else AN if i in apart else VM for i in range(len(args))],
        out_specs=[AN if i in out_apart else VM for i in range(len(outs))],
        scratch_shapes=list(scratch),
        compiler_params=pltpu.CompilerParams(vmem_limit_bytes=limit),
        cost_estimate=pl.CostEstimate(flops=flops, bytes_accessed=moved, transcendentals=0),
    )(*args)


def body(rhs, damping, omega, jac_diag, jac_face, face_list, stream_sends, cross_sends):
    count, rows, blocksize = rhs.shape
    columns = 2 * blocksize
    size = NVAR * NP * NP
    slots = count * FACES
    ss, sc = stream_sends.shape[-1], cross_sends.shape[-1]
    devices = lax.axis_size("stream") * lax.axis_size("cross")
    picks = np.zeros((FACES * size, rows), np.float32)
    picks[np.arange(FACES * size), face_rows()] = 1.0
    picks = jnp.asarray(picks, BF16)
    square = ((blocksize, blocksize), F32)
    field_out = ((count * rows, columns), F32)
    rhs = rhs.reshape(count * rows, blocksize)
    stage = [
        field_out,
        ((slots, size, columns), BF16),
        ((ss, size, columns), BF16),
        ((ss, size, columns), BF16),
        ((sc, size, columns), BF16),
        ((sc, size, columns), BF16),
        square,
        square,
    ]

    (gram,) = call(start_gram_kernel, "start_gram", [rhs, damping], [square])
    gram = total(gram)
    cells = float(devices * count * rows)
    field, traces, s0, s1, c0, c1, upper, inverse, center = call(
        functools.partial(start_kernel, cells),
        "start",
        [gram, rhs, picks, stream_sends, cross_sends],
        stage + [((8, blocksize), F32)],
        [],
        (3, 4),
    )
    basis, uppers, inverses, shifts, reduced = [field], [upper], [inverse], [], []
    chains = []
    for step in range(ITERS):
        from_prev = passed_along(s0, "stream", 1)
        from_next = passed_along(s1, "stream", -1)
        cross_prev = shifted(c0, "cross", 1)
        cross_next = shifted(c1, "cross", -1)
        part, shift, *chains = call(
            inner_kernel,
            "inner",
            [omega, center, damping, jac_diag, field, upper, inverse] + chains,
            [field_out, square, square, square],
            (),
            (0,),
            10**9,
        )
        shifts.append(shift)
        if step == ITERS - 1:
            (known,) = call(
                square_kernel,
                "square",
                reduced + shifts + [uppers[0], inverses[1], inverses[2]],
                [((8, blocksize, blocksize), F32)],
                (),
                (),
                10**9,
            )
        wide = (blocksize, (step + 2) * blocksize)
        sums_out = ((step + 2) * blocksize, blocksize)
        if step == 1:
            sums_out = (4 * blocksize, blocksize)
            if blocksize % devices == 0:
                sums_out = (devices, blocksize // devices, wide[1])
        image, sums = call(
            functools.partial(outer_kernel, step),
            "outer",
            [face_list, traces, from_prev, from_next, cross_prev, cross_next, jac_face, part]
            + basis,
            [field_out, (sums_out, F32)],
            [
                pltpu.VMEM((slots + 2 * ss + 2 * sc + 1, size, columns), BF16),
                pltpu.VMEM((FACES * size, columns), BF16),
                pltpu.VMEM(wide, F32),
            ],
            (0,),
        )
        sums = total(sums)
        if step < ITERS - 1:
            reduced.append(sums)
            field, traces, s0, s1, c0, c1, upper, inverse = call(
                functools.partial(next_kernel, step),
                "next",
                [sums, image] + basis + [picks, stream_sends, cross_sends],
                stage,
                [],
                (step + 4, step + 5),
            )
            basis.append(field)
            uppers.append(upper)
            inverses.append(inverse)
    out = ((count * rows, blocksize), F32)
    results = call(
        final_kernel,
        "final",
        [sums, image] + basis + [known],
        [out, out],
        [
            pltpu.VMEM((4,) + field_out[0], F32),
            pltpu.VMEM((8, blocksize, blocksize), F32),
            pltpu.VMEM(*out),
            pltpu.VMEM(*out),
            pltpu.SemaphoreType.DMA((5,)),
            pltpu.SemaphoreType.DMA((2, count)),
        ],
        (),
        0,
        None,
        range(1, 6),
        (0, 1),
    )
    return tuple(item.reshape(count, rows, blocksize) for item in results)


def solution(mesh):
    in_specs = (
        P(("stream", "cross"), None, None),
        P(("stream", "cross"), None),
        P(),
        P(("stream", "cross"), None, None),
        P(("stream", "cross"), None, None),
        P(("stream", "cross"), None),
        P(("stream", "cross"), None, None),
        P(("stream", "cross"), None, None),
    )
    out_specs = (P(("stream", "cross"), None, None), P(("stream", "cross"), None, None))
    return jax.shard_map(body, mesh=mesh, in_specs=in_specs, out_specs=out_specs, check_vma=False)
```

```python
import functools
import jax
import jax.numpy as jnp
import numpy as np
from jax import lax
from jax.experimental import pallas as pl
from jax.experimental.pallas import tpu as pltpu
from jax.sharding import PartitionSpec as P

NP = 4
NVAR = 5
ITERS = 3
FACES = 6
AXES = ("stream", "cross")
HIGH = lax.Precision.HIGHEST
F32 = jnp.float32
BF16 = jnp.bfloat16
LANES = 128
NEAR = 4
VMEM_LIMIT = 20 * 2**20


def passed_along(value, axis, steps):
    count = lax.axis_size(axis)
    first, last = (max(0, -steps), min(count, count - steps))
    return lax.ppermute(value, axis, [(source, source + steps) for source in range(first, last)])


def shifted(block, axis, distance):
    devices = range(lax.axis_size(axis))
    route = [((i - distance) % len(devices), i) for i in devices]
    return lax.ppermute(block, axis, route)


def total(block):
    count = lax.axis_size(AXES[0]) * lax.axis_size(AXES[1])
    if block.ndim == 3:
        return exchange(block)
    rows, width = block.shape
    share = -(-rows // count)
    if share * count != rows:
        block = jnp.pad(block, ((0, share * count - rows), (0, 0)))
    return exchange(block.reshape(count, share, width)).reshape(count * share, width)[:rows]


def exchange(shares):
    parts = lax.all_to_all(shares, AXES, 0, 0)
    (mine,) = call(add_up_kernel, "add_up", [parts], [(parts.shape, F32)], limit=4 * 2**20)
    return lax.all_to_all(mine, AXES, 0, 0)


def mm(left, right):
    return jnp.dot(left, right, precision=HIGH, preferred_element_type=F32)


def mm_tn(left, right):
    return lax.dot_general(
        left, right, (((0,), (0,)), ((), ())), precision=HIGH, preferred_element_type=F32
    )


def mm_nt(left, right):
    return lax.dot_general(
        left, right, (((1,), (1,)), ((), ())), precision=HIGH, preferred_element_type=F32
    )


def grid_of(shape, axis):
    return lax.broadcasted_iota(jnp.int32, shape, axis)


def identity(size):
    return jnp.where(grid_of((size, size), 0) == grid_of((size, size), 1), 1.0, 0.0).astype(F32)


def pivot_block(corner):
    size = corner.shape[0]
    columns = [jnp.broadcast_to(corner[:, t : t + 1], (size, LANES)) for t in range(size)]
    left = [[jnp.broadcast_to(columns[j][i : i + 1], (size, LANES)) for j in range(i + 1)] for i in range(size)]
    lower = [[None] * size for _ in range(size)]
    scales = []
    for j in range(size):
        scales.append(lax.rsqrt(left[j][j]))
        for i in range(j + 1, size):
            lower[i][j] = left[i][j] * scales[j]
        for i in range(j + 1, size):
            for k in range(j + 1, i + 1):
                left[i][k] = left[i][k] - lower[i][j] * lower[k][j]
    return lower, scales


def factor(gram):
    size = gram.shape[0]
    step = 8
    unit = identity(size)
    sides = [[m[r : r + step] for r in range(0, size, step)] for m in (gram, unit)]
    row = grid_of((step, size), 0)
    for p in range(size // step):
        base = p * step
        lower, scales = pivot_block(sides[0][p][:, base : base + step])
        leads = []
        for side in sides:
            rows = [jnp.broadcast_to(side[p][t : t + 1], (step, size)) for t in range(step)]
            for t in range(step):
                rows[t] = rows[t] * scales[t]
                for u in range(t + 1, step):
                    rows[u] = rows[u] - lower[u][t] * rows[t]
            strip = rows[0]
            for t in range(1, step):
                strip = jnp.where(row == t, rows[t], strip)
            side[p] = strip
            leads.append(rows)
        far = min(p + 1 + NEAR, size // step)
        for q in range(p + 1, far):
            strip = sides[0][q]
            columns = [jnp.broadcast_to(strip[:, base + t : base + t + 1], (step, size)) for t in range(step)]
            for t in range(step):
                share = columns[t] * scales[t]
                for u in range(t + 1, step):
                    columns[u] = columns[u] - share * lower[u][t]
                for side, lead in zip(sides, leads):
                    side[q] = side[q] - share * lead[t]
        if far * step < size:
            done = jnp.concatenate([side[p] for side in sides], 1)
            update = mm_tn(done[:, far * step : size], done)
            for q in range(far, size // step):
                at = (q - far) * step
                for k, side in enumerate(sides):
                    side[q] = side[q] - update[at : at + step, k * size : (k + 1) * size]
    upper = jnp.concatenate(sides[0], 0)
    upper = jnp.where(grid_of((size, size), 1) >= grid_of((size, size), 0), upper, 0.0)
    return upper, jnp.concatenate(sides[1], 0)


def rows_of(element, rows):
    return pl.ds(pl.multiple_of(element * rows, rows), rows)


def lanes_of(half, width):
    return pl.ds(pl.multiple_of(half * width, width), width)


def blocks_of(ref, count):
    if len(ref.shape) == 2:
        size = ref.shape[-1]
        return [ref[j * size : (j + 1) * size, :] for j in range(count)]
    size = ref.shape[-1] // count
    wide = ref[...].reshape(size, count * size)
    return [wide[:, j * size : (j + 1) * size] for j in range(count)]


def split(value):
    high = value.astype(BF16)
    return high, (value - high.astype(F32)).astype(BF16)


def pieces_of(matrix):
    high, low = split(matrix)
    both = jnp.concatenate([high, low], 1)
    return jnp.concatenate([both, both], 0)


def mm_pieces(parts, weights):
    pairs = [split(part) for part in parts]
    left = jnp.concatenate([p[0] for p in pairs] + [p[1] for p in pairs], 1)
    out = jnp.dot(left, weights, preferred_element_type=F32)
    size = out.shape[1] // 2
    return out[:, :size] + out[:, size:]


def thirds_of(matrix):
    high, low = split(matrix)
    rest = (matrix - high.astype(F32) - low.astype(F32)).astype(BF16)
    both = jnp.concatenate([high, low], 1)
    last = jnp.concatenate([high, jnp.zeros_like(high)], 1)
    return jnp.concatenate([both, both, last], 0), rest


def mm_thirds(parts, weights):
    weights, rest = weights
    pairs = [split(part) for part in parts]
    thirds = [
        (part - p[0].astype(F32) - p[1].astype(F32)).astype(BF16) for part, p in zip(parts, pairs)
    ]
    high = [p[0] for p in pairs]
    left = jnp.concatenate(high + [p[1] for p in pairs] + thirds, 1)
    out = jnp.dot(left, weights, preferred_element_type=F32)
    tail = jnp.dot(jnp.concatenate(high, 1), rest, preferred_element_type=F32)
    size = out.shape[1] // 2
    return out[:, :size] + (out[:, size:] + tail)


def take_traces(element, rows, picks_ref, field_ref, traces_ref):
    size = traces_ref.shape[1]
    rounded = field_ref[rows_of(element, rows), :].astype(BF16)
    picked = jnp.dot(picks_ref[...], rounded, preferred_element_type=F32).astype(BF16)
    for face in range(FACES):
        traces_ref[element * FACES + face] = picked[face * size : (face + 1) * size, :]


def pack(sends_ref, traces_ref, out_refs):
    for row, out_ref in enumerate(out_refs):
        for item in range(out_ref.shape[0]):
            out_ref[item] = traces_ref[sends_ref[0, row, item]]


def add_up_kernel(parts_ref, out_ref):
    out_ref[...] = jnp.broadcast_to(jnp.sum(parts_ref[...], axis=0, keepdims=True), out_ref.shape)


def start_gram_kernel(rhs_ref, damping_ref, out_ref):
    width = rhs_ref.shape[-1]
    both = jnp.concatenate(split(rhs_ref[...]), 1)
    gram = lax.dot_general(both, both, (((0,), (0,)), ((), ())), preferred_element_type=F32)
    gram = gram[:width] + gram[width:]
    gram = gram[:, :width] + gram[:, width:]
    mass = jnp.sum(jnp.sum(damping_ref[...], axis=1, keepdims=True), axis=0, keepdims=True)
    corner = (grid_of(gram.shape, 0) == width - 1) & (grid_of(gram.shape, 1) == 0)
    out_ref[...] = jnp.where(corner, mass, gram)


def start_kernel(
    cells, gram_ref, rhs_ref, picks_ref, ssend_ref, csend_ref,
    field_ref, traces_ref, s0_ref, s1_ref, c0_ref, c1_ref, upper_ref, inverse_ref, center_ref,
):
    width = rhs_ref.shape[-1]
    half = width // 2
    count = traces_ref.shape[0] // FACES
    rows = rhs_ref.shape[0] // count
    raw = gram_ref[...]
    r, c = grid_of(raw.shape, 0), grid_of(raw.shape, 1)
    corner = (r == width - 1) & (c == 0)
    mass = raw[width - 1 : width, 0:1]
    raw = jnp.where(corner, raw[0:1, width - 1 : width], raw)
    center_ref[...] = jnp.broadcast_to(mass * (1.0 / cells), center_ref.shape)
    rr, ri = raw[:half, :half], raw[:half, half:]
    ir, ii = raw[half:, :half], raw[half:, half:]
    same, other = rr + ii, ir - ri
    gram = jnp.concatenate(
        [jnp.concatenate([same, other], 1), jnp.concatenate([-other, same], 1)], 0
    )
    upper, inverse = factor(gram)
    upper_ref[...] = upper
    inverse_ref[...] = inverse
    turn = inverse.T
    first = jnp.concatenate([turn[:half], -turn[half:]], 0)
    second = jnp.concatenate([turn[half:], turn[:half]], 0)
    weights = thirds_of(first), thirds_of(second)

    @pl.loop(0, count)
    def _(e):
        field = [mm_thirds([rhs_ref[rows_of(e, rows), :]], item) for item in weights]
        field_ref[rows_of(e, rows), :] = jnp.concatenate(field, 1)
        take_traces(e, rows, picks_ref, field_ref, traces_ref)

    pack(ssend_ref, traces_ref, (s0_ref, s1_ref))
    pack(csend_ref, traces_ref, (c0_ref, c1_ref))


def next_kernel(
    level, red_ref, image_ref, *refs,
):
    basis = refs[: level + 1]
    picks_ref, ssend_ref, csend_ref = refs[level + 1 : level + 4]
    field_ref, traces_ref, s0_ref, s1_ref, c0_ref, c1_ref, upper_ref, inverse_ref = refs[level + 4 :]
    width = image_ref.shape[-1] // 2
    blocks = blocks_of(red_ref, level + 2)
    coeffs = jnp.concatenate(blocks[:-1], 1)
    gram = blocks[-1] - mm_nt(coeffs, coeffs)
    upper, inverse = factor(gram)
    upper_ref[...] = upper
    inverse_ref[...] = inverse
    turn = inverse.T
    weights = thirds_of(jnp.concatenate([turn, -mm_tn(coeffs, turn)], 0))
    count = traces_ref.shape[0] // FACES
    rows = field_ref.shape[0] // count

    @pl.loop(0, count)
    def _(e):
        at = rows_of(e, rows)
        for h in range(2):
            cut = slice(h * width, (h + 1) * width)
            parts = [ref[at, cut] for ref in (image_ref,) + basis]
            field_ref[at, cut] = mm_thirds(parts, weights)
        take_traces(e, rows, picks_ref, field_ref, traces_ref)

    pack(ssend_ref, traces_ref, (s0_ref, s1_ref))
    pack(csend_ref, traces_ref, (c0_ref, c1_ref))


def turned(matrix):
    half = matrix.shape[0] // 2
    return jnp.concatenate([-matrix[half:], matrix[:half]], 0)


def inner_kernel(
    omega_ref, center_ref, damping_ref, diag_ref, field_ref, upper_ref, inverse_ref, *refs,
):
    part_ref, shift_ref, chain_out, unchain_out = refs[-4:]
    chain_refs = refs[:-4]
    chain, unchain = upper_ref[...], inverse_ref[...].T
    if chain_refs:
        chain = mm(chain, chain_refs[0][...])
        unchain = mm(chain_refs[1][...], unchain)
    chain_out[...] = chain
    unchain_out[...] = unchain
    omega = omega_ref[0]
    center = center_ref[0:1, 0:1]
    twist = omega * mm(chain, turned(unchain))
    shift_ref[...] = (twist + center * identity(twist.shape[0])).T
    width = twist.shape[0]
    rows = diag_ref.shape[1]

    @pl.loop(0, diag_ref.shape[0])
    def _(e):
        at = rows_of(e, rows)
        re, im = field_ref[at, :width], field_ref[at, width:]
        local = jnp.dot(diag_ref[e], field_ref[at, :].astype(BF16), preferred_element_type=F32)
        scale = jnp.swapaxes(damping_ref[pl.ds(e, 1), :] - center, 0, 1)
        part_ref[at, :width] = local[:, :width] + scale * re - omega * im - mm(re, twist)
        part_ref[at, width:] = local[:, width:] + scale * im + omega * re - mm(im, twist)


def square_kernel(
    sums0_ref, sums1_ref, shift0_ref, shift1_ref, shift2_ref, s0_ref, i1_ref, i2_ref, pack_ref,
):
    width = s0_ref.shape[0]
    t00 = sums0_ref[:width, :] + shift0_ref[...]
    t01, t11, _ = blocks_of(sums1_ref, 3)
    t11 = t11 + shift1_ref[...]
    n1 = -mm(i1_ref[...], t00)
    n2 = -mm(i2_ref[...], t01 + mm(t11, n1))
    gram = identity(width) + mm_tn(n1, n1) + mm_tn(n2, n2)
    _, inverse = factor(gram)
    turn = inverse.T
    items = (turn, mm(n1, turn), mm(n2, turn), mm(inverse, s0_ref[...]), i1_ref[...], i2_ref[...])
    for at, item in enumerate(items + (mm_tn(i1_ref[...], t11.T), shift2_ref[...])):
        pack_ref[at] = item


def outer_kernel(level, list_ref, traces_ref, prev_ref, next_ref, cprev_ref, cnext_ref,
                 face_ref, part_ref, *refs):
    basis = refs[: level + 1]
    image_ref, out_ref, table, nearby, total_ref = refs[level + 1 :]
    own = traces_ref.shape[0]
    size = traces_ref.shape[1]
    at = 0
    for ref in (traces_ref, prev_ref, next_ref, cprev_ref, cnext_ref):
        table[at : at + ref.shape[0]] = ref[...]
        at += ref.shape[0]
    table[at] = jnp.zeros(table.shape[1:], table.dtype)
    count, rows = face_ref.shape[:2]
    width = part_ref.shape[-1] // 2

    @pl.loop(0, count)
    def _(e):
        for f in range(FACES):
            nearby[f * size : (f + 1) * size, :] = table[list_ref[e, f]]
        coupled = jnp.dot(face_ref[e], nearby[...], preferred_element_type=F32)
        image_ref[rows_of(e, rows), :] = part_ref[rows_of(e, rows), :] + coupled

    sums_ref = out_ref if len(out_ref.shape) == 2 else total_ref
    sums_ref[...] = jnp.zeros_like(sums_ref)
    piece = 2 * width if (count * rows) % (2 * width) == 0 else rows

    @pl.loop(0, count * rows // piece)
    def _(i):
        lefts, rights = [], []
        for h in range(2):
            at = (rows_of(i, piece), slice(h * width, (h + 1) * width))
            parts = [split(ref[at]) for ref in basis + (image_ref,)]
            lefts += [jnp.concatenate(parts[-1], 1)] * 2
            rights += [jnp.concatenate([p[k] for p in parts], 1) for k in range(2)]
        term = lax.dot_general(
            jnp.concatenate(lefts, 0),
            jnp.concatenate(rights, 0),
            (((0,), (0,)), ((), ())),
            preferred_element_type=F32,
        )
        term = term[:width] + term[width:]
        if len(out_ref.shape) == 3:
            sums_ref[...] += term
        else:
            for j in range(level + 2):
                sums_ref[j * width : (j + 1) * width, :] += term[:, j * width : (j + 1) * width]

    if len(out_ref.shape) == 3:
        out_ref[...] = sums_ref[...].reshape(out_ref.shape)


def final_kernel(
    red_ref, image_ref, v0_ref, v1_ref, v2_ref, pack_ref, solution_ref, residual_ref,
    fields, small, solved, left_over, in_sems, out_sems,
):
    load = pltpu.make_async_copy(pack_ref, small, in_sems.at[4])
    load.start()
    loads = [
        pltpu.make_async_copy(ref, fields.at[j], in_sems.at[j])
        for j, ref in enumerate((v0_ref, v1_ref, v2_ref, image_ref))
    ]
    for copy in loads:
        copy.start()
    width = red_ref.shape[-1]
    half = width // 2
    blocks = [red_ref[j * width : (j + 1) * width, :] for j in range(4)]
    coeffs = jnp.concatenate(blocks[:-1], 1)
    gram = blocks[-1] - mm_nt(coeffs, coeffs)
    load.wait()
    reach_in = small[0:3].reshape(3 * width, width)
    right, i1, i2, mixed, shift2 = [small[k] for k in range(3, 8)]
    shifted_coeffs = jnp.concatenate([coeffs[:, : 2 * width], coeffs[:, 2 * width :] + shift2], 1)
    reach = mm(shifted_coeffs, reach_in)
    goal = mm(reach, right)
    _, iq = factor(gram + mm_nt(reach, reach))
    y2 = mm_tn(iq, mm(iq, goal))
    z = mm_pieces([reach_in], pieces_of(right - mm_tn(reach, y2)))
    z = [z[k * width : (k + 1) * width] for k in range(3)]
    hy = mm_tn(jnp.concatenate([coeffs, shift2], 1), y2)
    hy = [hy[k * width : (k + 1) * width] for k in range(4)]
    y1 = -mm_tn(i2, z[2] + hy[2] + hy[3])
    y0 = -mm_tn(i1, z[1] + hy[1]) - mm_pieces([mixed], pieces_of(y1))
    left = grid_of((width, width), 1) < half
    rows = []
    for y, w in ((y0, z[0] + hy[0]), (y1, z[1] + hy[1]), (y2, z[2] + hy[2]), (0.0 * y2, -y2)):
        rows.append(jnp.where(left, y, pltpu.roll(w, half, 1)))
    weights = pieces_of(jnp.concatenate(rows, 0))
    count = out_sems.shape[1]
    size = solved.shape[0] // count
    lanes = grid_of((size, width), 1) < half
    for copy in loads:
        copy.wait()

    def copies(e):
        at = rows_of(e, size)
        return [
            pltpu.make_async_copy(solved.at[at], solution_ref.at[at], out_sems.at[0, e]),
            pltpu.make_async_copy(left_over.at[at], residual_ref.at[at], out_sems.at[1, e]),
        ]

    @pl.loop(0, count)
    def _(e):
        at = rows_of(e, size)

        parts = [
            jnp.concatenate([fields[j, at, :width], fields[j, at, width:]], 0) for j in range(4)
        ]
        out = mm_pieces(parts, weights)
        first, second = out[:size], out[size:]
        solved[at, :] = jnp.where(lanes, first, pltpu.roll(second, half, 1))
        left_over[at, :] = jnp.where(lanes, pltpu.roll(first, half, 1), second)
        for copy in copies(e):
            copy.start()

    for e in range(count):
        for copy in copies(e):
            copy.wait()


def face_rows():
    grid = np.arange(NVAR * NP * NP * NP).reshape(NVAR, NP, NP, NP)
    faces = [
        grid[:, 0],
        grid[:, NP - 1],
        grid[:, :, 0],
        grid[:, :, NP - 1],
        grid[:, :, :, 0],
        grid[:, :, :, NP - 1],
    ]
    return np.concatenate([item.reshape(-1) for item in faces]).astype(np.int32)


VM = pl.BlockSpec(memory_space=pltpu.VMEM)
SM = pl.BlockSpec(memory_space=pltpu.SMEM)
AN = pl.BlockSpec(memory_space=pl.ANY)


def call(
    kernel, name, args, outs, scratch=(), scalars=(), flops=0, limit=VMEM_LIMIT, apart=(), out_apart=()
):
    moved = sum(a.size * a.dtype.itemsize for a in args)
    return pl.pallas_call(
        kernel,
        name=name,
        out_shape=[jax.ShapeDtypeStruct(shape, dtype) for shape, dtype in outs],
        in_specs=[SM if i in scalars else AN if i in apart else VM for i in range(len(args))],
        out_specs=[AN if i in out_apart else VM for i in range(len(outs))],
        scratch_shapes=list(scratch),
        compiler_params=pltpu.CompilerParams(vmem_limit_bytes=limit),
        cost_estimate=pl.CostEstimate(flops=flops, bytes_accessed=moved, transcendentals=0),
    )(*args)


def body(rhs, damping, omega, jac_diag, jac_face, face_list, stream_sends, cross_sends):
    count, rows, blocksize = rhs.shape
    columns = 2 * blocksize
    size = NVAR * NP * NP
    slots = count * FACES
    ss, sc = stream_sends.shape[-1], cross_sends.shape[-1]
    devices = lax.axis_size("stream") * lax.axis_size("cross")
    picks = np.zeros((FACES * size, rows), np.float32)
    picks[np.arange(FACES * size), face_rows()] = 1.0
    picks = jnp.asarray(picks, BF16)
    square = ((blocksize, blocksize), F32)
    field_out = ((count * rows, columns), F32)
    rhs = rhs.reshape(count * rows, blocksize)
    stage = [
        field_out,
        ((slots, size, columns), BF16),
        ((ss, size, columns), BF16),
        ((ss, size, columns), BF16),
        ((sc, size, columns), BF16),
        ((sc, size, columns), BF16),
        square,
        square,
    ]

    (gram,) = call(start_gram_kernel, "start_gram", [rhs, damping], [square])
    gram = total(gram)
    cells = float(devices * count * rows)
    field, traces, s0, s1, c0, c1, upper, inverse, center = call(
        functools.partial(start_kernel, cells),
        "start",
        [gram, rhs, picks, stream_sends, cross_sends],
        stage + [((8, blocksize), F32)],
        [],
        (3, 4),
    )
    basis, uppers, inverses, shifts, reduced = [field], [upper], [inverse], [], []
    chains = []
    for step in range(ITERS):
        from_prev = passed_along(s0, "stream", 1)
        from_next = passed_along(s1, "stream", -1)
        cross_prev = shifted(c0, "cross", 1)
        cross_next = shifted(c1, "cross", -1)
        part, shift, *chains = call(
            inner_kernel,
            "inner",
            [omega, center, damping, jac_diag, field, upper, inverse] + chains,
            [field_out, square, square, square],
            (),
            (0,),
            10**9,
        )
        shifts.append(shift)
        if step == ITERS - 1:
            (known,) = call(
                square_kernel,
                "square",
                reduced + shifts + [uppers[0], inverses[1], inverses[2]],
                [((8, blocksize, blocksize), F32)],
                (),
                (),
                10**9,
            )
        wide = (blocksize, (step + 2) * blocksize)
        sums_out = ((step + 2) * blocksize, blocksize)
        if step == 1:
            sums_out = (4 * blocksize, blocksize)
            if blocksize % devices == 0:
                sums_out = (devices, blocksize // devices, wide[1])
        image, sums = call(
            functools.partial(outer_kernel, step),
            "outer",
            [face_list, traces, from_prev, from_next, cross_prev, cross_next, jac_face, part]
            + basis,
            [field_out, (sums_out, F32)],
            [
                pltpu.VMEM((slots + 2 * ss + 2 * sc + 1, size, columns), BF16),
                pltpu.VMEM((FACES * size, columns), BF16),
                pltpu.VMEM(wide, F32),
            ],
            (0,),
        )
        sums = total(sums)
        if step < ITERS - 1:
            reduced.append(sums)
            field, traces, s0, s1, c0, c1, upper, inverse = call(
                functools.partial(next_kernel, step),
                "next",
                [sums, image] + basis + [picks, stream_sends, cross_sends],
                stage,
                [],
                (step + 4, step + 5),
            )
            basis.append(field)
            uppers.append(upper)
            inverses.append(inverse)
    out = ((count * rows, blocksize), F32)
    results = call(
        final_kernel,
        "final",
        [sums, image] + basis + [known],
        [out, out],
        [
            pltpu.VMEM((4,) + field_out[0], F32),
            pltpu.VMEM((8, blocksize, blocksize), F32),
            pltpu.VMEM(*out),
            pltpu.VMEM(*out),
            pltpu.SemaphoreType.DMA((5,)),
            pltpu.SemaphoreType.DMA((2, count)),
        ],
        (),
        0,
        None,
        range(1, 6),
        (0, 1),
    )
    return tuple(item.reshape(count, rows, blocksize) for item in results)


def solution(mesh):
    in_specs = (
        P(("stream", "cross"), None, None),
        P(("stream", "cross"), None),
        P(),
        P(("stream", "cross"), None, None),
        P(("stream", "cross"), None, None),
        P(("stream", "cross"), None),
        P(("stream", "cross"), None, None),
        P(("stream", "cross"), None, None),
    )
    out_specs = (P(("stream", "cross"), None, None), P(("stream", "cross"), None, None))
    return jax.shard_map(body, mesh=mesh, in_specs=in_specs, out_specs=out_specs, check_vma=False)
```
